512 devices in a mesh: region: 32 (over x, y), shard: 16 (over z, core).
Axes of the slice: x: 4, y: 8, z: 8, core: 2. Of those that a mesh axis runs over, the one named last changes fastest.
Arguments:
- state_anom: float32 [524288, 256], P(('region', 'shard')), may hold values from -6 to 6
- state_mean: float32 [524288], P(('region', 'shard')), may hold values from -6 to 6
- obs_anom: float32 [64, 512, 256], P('region', 'shard'), may hold values from -6 to 6
- obs_depart: float32 [64, 512], P('region', 'shard'), may hold values from -6 to 6
- obs_var: float32 [64, 512], P('region', 'shard'), may hold values from 0.5 to 2
- taper_levels: float32 [8], replicated, may hold values from 0 to 1
- state_taper: int32 [4096, 256], P(('region', 'shard')), may hold values from 0 to 7
- obs_taper: int32 [256, 256], P('region'), may hold values from 0 to 7
- batch_order: int32 [3], replicated, may hold values from 0 to 63, as said below
Outputs:
- post_anom: float32 [524288, 256], P(('region', 'shard'))
- post_mean: float32 [524288], P(('region', 'shard'))
- post_obs_anom: float32 [64, 512, 256], P('region', 'shard')
- post_obs_depart: float32 [64, 512], P('region', 'shard')
The draws below stay inside these ranges and needn't reach their ends.
Inputs may be any that keep to these rules, and one draw needn't show every extreme that they name: `batch_order`: 3 distinct batch numbers; batch q lies in region q // 2; the first and the last batch number both occur.
All inputs are finite; a program needn't handle non-finite values.
Results may differ from the reference program's by a relative error of at most 0.0001.
Values sent between devices are 32-bit elements; how exact they have to be, the bound alone decides.
No kernel may reach another device: no remote copies, remote signals or barrier semaphores. Data moves between devices by JAX's collectives and lax.ppermute only.
A program may use at most 64 MiB of HBM per device.

```python
import math
import jax
import jax.numpy as jnp
from jax import lax

M = 256
P_SIZE = 512
TAPER_BLOCK = 128
LEVELS = 8
NB = 3
ROWS_DEV = 1024
STATE = 524288
NOBSB = 64
NOBS = 32768


def draw_batch_order(key, part):
    inner = jax.random.permutation(jax.random.fold_in(key, 11), NOBSB - 2)[:NB - 2] + 1
    chosen = jnp.concatenate([jnp.array([0, NOBSB - 1], jnp.int32), inner.astype(jnp.int32)])
    return jax.random.permutation(jax.random.fold_in(key, 12), chosen).astype(jnp.int32)


def place_ends(result, stream_key, least, largest):
    place = [jax.random.randint(jax.random.fold_in(stream_key, axis), (), 0, length) for axis, length in enumerate(result.shape)]
    widest = result.shape.index(max(result.shape))
    neighbour = place[:widest] + [(place[widest] + 1) % result.shape[widest]] + place[widest + 1:]
    return result.at[tuple(place)].set(least).at[tuple(neighbour)].set(largest)


def block_levels(key, dims, cuts, least, largest):
    def one(axis_at, blocks):
        heights = jax.random.uniform(jax.random.fold_in(jax.random.fold_in(key, 6), axis_at), (blocks,), jnp.float32, least / len(cuts), largest / len(cuts))
        return jnp.repeat(jnp.exp(heights), dims[axis_at] // blocks).reshape((-1,) + (1,) * (len(dims) - axis_at - 1))

    level = one(*cuts[0])
    for cut in cuts[1:]:
        level = level * one(*cut)
    return level


def gaussian(rng, shape, deviation, bound, cuts=(), held_as=jnp.bfloat16):
    drawn = deviation * jax.random.normal(rng, shape, jnp.float32)
    if cuts:
        drawn = drawn * block_levels(rng, shape, cuts, -0.22, 0.18)
    return jnp.clip(drawn, -bound, bound).astype(held_as)


def setup_inputs(seed: int = 0) -> dict:
    keys = jax.random.split(jax.random.key(seed), 10)
    state_anom = gaussian(keys[0], (STATE, M), 1.0, 6.0, ((0, 512),), jnp.float32)
    state_mean = gaussian(keys[1], (STATE,), 1.0, 6.0, ((0, 512),), jnp.float32)
    obs_anom = gaussian(keys[2], (NOBSB, P_SIZE, M), 1.0, 6.0, ((0, 32), (1, 16)), jnp.float32)
    obs_depart = gaussian(keys[3], (NOBSB, P_SIZE), 1.0, 6.0, ((0, 32), (1, 16)), jnp.float32)
    obs_var = jnp.clip(jnp.exp(math.log(2.0) - 1.3862944 * jax.random.uniform(keys[4], (NOBSB, P_SIZE), jnp.float32) ** block_levels(keys[4], (NOBSB, P_SIZE), ((0, 32), (1, 16)), -0.2, 0.2)), 0.5, 2.0)
    taper_levels = jnp.clip(jax.random.uniform(keys[5], (LEVELS,), jnp.float32, 0.0, 1.0), 0.0, 1.0)
    state_taper = place_ends(jax.random.randint(keys[6], (STATE // TAPER_BLOCK, NOBS // TAPER_BLOCK), 0, LEVELS), jax.random.fold_in(keys[6], 1), 0, LEVELS - 1).astype(jnp.int32)
    obs_taper = place_ends(jax.random.randint(keys[7], (NOBS // TAPER_BLOCK, NOBS // TAPER_BLOCK), 0, LEVELS), jax.random.fold_in(keys[7], 1), 0, LEVELS - 1).astype(jnp.int32)
    batch_order = draw_batch_order(jax.random.fold_in(keys[9], 71), 0)
    return dict(state_anom=state_anom, state_mean=state_mean, obs_anom=obs_anom, obs_depart=obs_depart, obs_var=obs_var, taper_levels=taper_levels, state_taper=state_taper, obs_taper=obs_taper, batch_order=batch_order)


highest = lax.Precision.HIGHEST

def factorize(anomalies, departs, variances):
    product = jnp.dot(anomalies.astype(jnp.float32), anomalies.T.astype(jnp.float32), precision=highest, preferred_element_type=jnp.float32)
    system = product / (M - 1) + jnp.diag(variances)
    lower_factor = jnp.linalg.cholesky(system)
    shifted = lower_factor + jnp.diag(jnp.sqrt(variances))
    solved = lax.linalg.triangular_solve(shifted, anomalies, left_side=True, lower=True)
    increments = lax.linalg.triangular_solve(lower_factor, solved, left_side=True, lower=True, transpose_a=True)
    first = lax.linalg.triangular_solve(lower_factor, departs[:, None], left_side=True, lower=True)
    weights = lax.linalg.triangular_solve(lower_factor, first, left_side=True, lower=True, transpose_a=True)
    return (increments, weights[:, 0])

def regress(rows, batch_rows, taper, increments, weights):
    count_rows = rows.shape[0]
    blocks = P_SIZE // TAPER_BLOCK
    covar = jnp.dot(rows.astype(jnp.float32), batch_rows.T.astype(jnp.float32), precision=highest, preferred_element_type=jnp.float32) / (M - 1)
    covar = covar.reshape(count_rows // TAPER_BLOCK, TAPER_BLOCK, blocks, TAPER_BLOCK) * taper[:, None, :, None]
    covar = covar.reshape(count_rows, P_SIZE)
    delta_rows = jnp.dot(covar.astype(jnp.float32), increments.astype(jnp.float32), precision=highest, preferred_element_type=jnp.float32)
    delta_mean = jnp.dot(covar.astype(jnp.float32), weights.astype(jnp.float32), precision=highest, preferred_element_type=jnp.float32)
    return (delta_rows, delta_mean)

def reference(state_anom, state_mean, obs_anom, obs_depart, obs_var, taper_levels, state_taper, obs_taper, batch_order):
    blocks = P_SIZE // TAPER_BLOCK
    groups = STATE // ROWS_DEV
    anomaly = state_anom.reshape(groups, ROWS_DEV, M)
    mean_state = state_mean.reshape(groups, ROWS_DEV)
    obs_now = obs_anom
    depart_now = obs_depart
    for section_idx in range(NB):
        batch_id = batch_order[section_idx]
        batch_rows = lax.dynamic_index_in_dim(obs_now, batch_id, 0, keepdims=False)
        departs = lax.dynamic_index_in_dim(depart_now, batch_id, 0, keepdims=False)
        variances = lax.dynamic_index_in_dim(obs_var, batch_id, 0, keepdims=False)
        increments, weights = factorize(batch_rows, departs, variances)
        state_cols = lax.dynamic_slice_in_dim(state_taper, batch_id * blocks, blocks, 1)
        state_weights = taper_levels[state_cols].reshape(groups, ROWS_DEV // TAPER_BLOCK, blocks)
        obs_cols = lax.dynamic_slice_in_dim(obs_taper, batch_id * blocks, blocks, 1)
        obs_weights = taper_levels[obs_cols].reshape(NOBSB, P_SIZE // TAPER_BLOCK, blocks)

        def state_group(items):
            rows, means, taper = items
            delta_rows, delta_mean = regress(rows, batch_rows, taper, increments, weights)
            return (rows - delta_rows, means + delta_mean)

        def obs_group(items):
            rows, departs_here, taper = items
            delta_rows, delta_mean = regress(rows, batch_rows, taper, increments, weights)
            return (rows - delta_rows, departs_here - delta_mean)
        anomaly, mean_state = lax.map(state_group, (anomaly, mean_state, state_weights))
        obs_now, depart_now = lax.map(obs_group, (obs_now, depart_now, obs_weights))
    return (anomaly.reshape(STATE, M), mean_state.reshape(STATE), obs_now, depart_now)
```

```python
import jax
import jax.numpy as jnp
from jax import lax
from jax.experimental import pallas as pl
from jax.experimental.pallas import tpu as pltpu
from jax.sharding import Mesh, PartitionSpec as P

M = 256
N = 512
B = 128
NBLK = N // B
NB = 3
KB = 2
XS, YS, ZS, CS = 4, 8, 8, 2
PIECE = 32
WIDE = M + B
HI = lax.Precision.HIGHEST
F32 = jnp.float32


def mm(a, b, ca=1, cb=0):
    return lax.dot_general(a, b, (((ca,), (cb,)), ((), ())), precision=HI, preferred_element_type=F32)


def iota(shape, axis):
    return lax.broadcasted_iota(jnp.int32, shape, axis)


def wide(v):
    return jnp.concatenate([v, v], axis=1)


def factor_block(a_ref, q_ref, w_ref):
    q_ref[...] = jnp.zeros_like(q_ref)
    for g in range(B // 8):
        j0 = 8 * g
        rows = [jnp.broadcast_to(a_ref[j0 + s : j0 + s + 1, :], (8, 2 * B)) for s in range(8)]
        d = {}
        for s in range(8):
            for t in range(s + 1):
                d[s, t] = jnp.broadcast_to(rows[t][:, j0 + s : j0 + s + 1], (8, B))
        inv, low, done = [], {}, []
        for t in range(8):
            inv.append(lax.rsqrt(d[t, t]))
            done.append(rows[t] * wide(inv[t]))
            for s in range(t + 1, 8):
                low[s, t] = d[s, t] * inv[t]
            for s in range(t + 1, 8):
                for v in range(t + 1, s + 1):
                    d[s, v] = d[s, v] - low[s, t] * low[v, t]
            for s in range(t + 1, 8):
                rows[s] = rows[s] - wide(low[s, t]) * done[t]
        for s in range(8):
            w_ref[j0 + s : j0 + s + 1, :] = done[s][:1, B:]
        if g == B // 8 - 1:
            break
        back = list(done)
        for t in range(7, -1, -1):
            back[t] = back[t] * wide(inv[t])
            for s in range(t):
                back[s] = back[s] - wide(low[t, s]) * back[t]
        if g:
            q_ref[j0 - 8 : j0, :] = jnp.zeros((8, 2 * B), F32)
        for s in range(8):
            q_ref[j0 + s : j0 + s + 1, :] = back[s][:1, :]
        lo = j0 + 8
        a_ref[lo:, :] = a_ref[lo:, :] - mm(a_ref[lo:, :B], q_ref[...])


def lower_inverses(ts):
    ri, ci = iota((B, B), 0), iota((B, B), 1)
    xs = [jnp.where(ri == ci, 1.0 / t, 0.0) for t in ts]
    m = 1
    while m < B:
        mask = (ri // (2 * m) == ci // (2 * m)) & ((ri // m) % 2 == 1) & ((ci // m) % 2 == 0)
        mid = [mm(jnp.where(mask, t, 0.0), x) for t, x in zip(ts, xs)]
        xs = [x - mm(x, y) for x, y in zip(xs, mid)]
        m *= 2
    return xs


def analysis_kernel(
    wts_ref, one_ref, two_ref, x_ref, mean_ref, obs_ref,
    xo_ref, meano_ref, obso_ref, depo_ref,
    y_ref, d_ref, r_ref, s_ref, u_ref, w_ref, a_ref, q_ref, v_ref, g_ref, dm_ref, do_ref,
):
    eye = iota((B, B), 0) == iota((B, B), 1)
    low_mask = iota((B, B), 0) >= iota((B, B), 1)
    piece_eye = iota((PIECE, B), 0) == iota((PIECE, B), 1)
    var_eye = iota((PIECE, B), 0) + PIECE == iota((PIECE, B), 1)
    shards = ZS * CS
    for s in range(shards):
        at = s * PIECE
        y_ref[0, at : at + 32, :] = one_ref[s, 0:32, :]
        y_ref[1, at : at + 32, :] = two_ref[s, 0:32, :]
        y_ref[2, at : at + 24, :] = two_ref[s, 32:56, :]
        y_ref[2, at + 24 : at + 32, :] = one_ref[s, 40:48, :]
        for k in range(NB):
            line = jnp.broadcast_to(one_ref[s, 32 + k : 33 + k, :B], (PIECE, B))
            for mask, ref in ((piece_eye, d_ref), (var_eye, r_ref)):
                col = jnp.sum(jnp.where(mask, line, 0.0), axis=1, keepdims=True)
                ref[k, at : at + PIECE, :] = jnp.broadcast_to(col, (PIECE, B))
    xo_ref[...] = x_ref[...]
    obso_ref[...] = obs_ref[...]
    dm_ref[...] = jnp.zeros_like(dm_ref)
    do_ref[...] = jnp.zeros_like(do_ref)

    for k in range(NB):
        s_ref[:, :N] = mm(y_ref[k], y_ref[k], 1, 1) * (1.0 / (M - 1))
        s_ref[:, N:] = d_ref[k]
        for b in range(NBLK):
            sl = slice(b * B, b * B + B)
            s_ref[sl, sl] = s_ref[sl, sl] + jnp.where(eye, r_ref[k, sl, :], 0.0)

        def block_step(b, carry):
            at = pl.multiple_of(b * B, B)
            a_ref[:, :B] = s_ref[pl.ds(at, B), pl.ds(at, B)]
            a_ref[:, B:] = jnp.where(eye, 1.0, 0.0)
            factor_block(a_ref, q_ref, w_ref.at[b])
            inv = w_ref[b]
            row = mm(inv, s_ref[pl.ds(at, B), :])
            u_ref[pl.ds(at, B), :] = row
            for c in range(NBLK - 1):
                @pl.when(b == c)
                def _():
                    lo = (c + 1) * B
                    q = mm(inv, u_ref[lo - B : lo, lo:], 0, 0)
                    s_ref[lo:, lo:] = s_ref[lo:, lo:] - mm(s_ref[lo:, lo - B : lo], q)
            return carry

        lax.fori_loop(0, NBLK, block_step, 0)

        shifted = []
        for b in range(NBLK):
            sl = slice(b * B, b * B + B)
            low = jnp.where(low_mask, jnp.transpose(u_ref[sl, sl]), 0.0)
            shifted.append(low + jnp.where(eye, jnp.sqrt(r_ref[k, sl, :]), 0.0))
        tinv = lower_inverses(shifted)

        v_ref[:, :M] = y_ref[k]
        v_ref[:, M:] = u_ref[:, N:]
        for b in range(NBLK):
            sl = slice(b * B, b * B + B)
            hi = (b + 1) * B
            v_ref[sl, :M] = mm(tinv[b], v_ref[sl, :M])
            if b < NBLK - 1:
                v_ref[hi:, :M] = v_ref[hi:, :M] - mm(u_ref[sl, hi:N], v_ref[sl, :M], 0, 0)
        for b in range(NBLK - 1, -1, -1):
            sl = slice(b * B, b * B + B)
            hi = (b + 1) * B
            rhs = v_ref[sl, :]
            if b < NBLK - 1:
                rhs = rhs - mm(u_ref[sl, hi:N], v_ref[hi:, :])
            v_ref[sl, :] = mm(w_ref[b], rhs, 0, 0)
        for b in range(NBLK):
            sl = slice(b * B, b * B + B)
            g_ref[b] = mm(y_ref[k, sl, :], v_ref[sl, :], 0, 0) * (1.0 / (M - 1))

        def gain(weight):
            total = weight(0) * g_ref[0]
            for j in range(1, NBLK):
                total = total + weight(j) * g_ref[j]
            return total

        for later in range(k + 1, NB):
            for i in range(NBLK):
                sl = slice(i * B, i * B + B)
                lane = 2 * PIECE + k * NBLK * NBLK + i * NBLK
                mat = gain(lambda j: one_ref[0, 32 + later : 33 + later, lane + j : lane + j + 1])
                delta = mm(y_ref[later, sl, :], mat)
                y_ref[later, sl, :] = y_ref[later, sl, :] - delta[:, :M]
                d_ref[later, sl, :] = d_ref[later, sl, :] - delta[:, M:]

        def state_step(i, carry):
            at = pl.multiple_of(i * B, B)
            mat = gain(lambda j: wts_ref[k, i, j])
            rows = xo_ref[pl.ds(at, B), :]
            delta = mm(rows, mat)
            xo_ref[pl.ds(at, B), :] = rows - delta[:, :M]
            dm_ref[pl.ds(at, B), :] = dm_ref[pl.ds(at, B), :] + delta[:, M:]
            return carry

        lax.fori_loop(0, x_ref.shape[0] // B, state_step, 0)
        for q in range(KB):
            sl = slice(q * PIECE, q * PIECE + PIECE)
            mat = gain(lambda j: wts_ref[k, x_ref.shape[0] // B + q, j])
            rows = obso_ref[sl, :]
            delta = mm(rows, mat)
            obso_ref[sl, :] = rows - delta[:, :M]
            do_ref[sl, :] = do_ref[sl, :] + delta[:, M:]

    for i in range(x_ref.shape[0] // B):
        sl = slice(i * B, i * B + B)
        add = jnp.sum(jnp.where(eye, dm_ref[sl, :], 0.0), axis=0, keepdims=True)
        meano_ref[i : i + 1, :] = mean_ref[i : i + 1, :] + add
    for q in range(KB):
        sl = slice(q * PIECE, q * PIECE + PIECE)
        sub = jnp.sum(jnp.where(piece_eye, do_ref[sl, :], 0.0), axis=0, keepdims=True)
        depo_ref[q : q + 1, :] = sub


def analysis(wts, one, two, x, mean, obs):
    shape = lambda *dims: jax.ShapeDtypeStruct(dims, F32)
    scratch = lambda *dims: pltpu.VMEM(dims, F32)
    vmem = pl.BlockSpec(memory_space=pltpu.VMEM)
    rows = x.shape[0]
    return pl.pallas_call(
        analysis_kernel,
        out_shape=[shape(rows, M), shape(rows // B, B), shape(KB * PIECE, M), shape(KB, B)],
        in_specs=[pl.BlockSpec(memory_space=pltpu.SMEM)] + [vmem] * 5,
        out_specs=[vmem] * 4,
        scratch_shapes=[
            scratch(NB, N, M),
            scratch(NB, N, B),
            scratch(NB, N, B),
            scratch(N, N + B),
            scratch(N, N + B),
            scratch(NBLK, B, B),
            scratch(B, 2 * B),
            scratch(B, 2 * B),
            scratch(N, WIDE),
            scratch(NBLK, M, WIDE),
            scratch(rows, B),
            scratch(KB * PIECE, B),
        ],
        name="analysis",
    )(wts, one, two, x, mean, obs)


def lookup(levels, index):
    onehot = index[..., None] == jnp.arange(levels.shape[0], dtype=jnp.int32)
    return jnp.sum(jnp.where(onehot, levels, 0.0), axis=-1)


def spread(block, roots, axis, size, per_row):
    place = lax.axis_index(axis)
    away = (place - roots + size) % size
    step = size // 2
    while step:
        moved = lax.ppermute(block, axis, [(i, (i + step) % size) for i in range(size)])
        keep = (away % (2 * step)) == 0
        block = jnp.where(per_row(keep), block, moved)
        step //= 2
    return block


def per_device(state_anom, state_mean, obs_anom, obs_depart, obs_var, taper_levels, state_taper, obs_taper, batch_order):
    shard = lax.axis_index("z") * CS + lax.axis_index("c")
    owner = batch_order // KB
    local = batch_order % KB
    pieces = [lax.dynamic_index_in_dim(obs_anom, local[k], 0, keepdims=False) for k in range(NB)]
    lines = []
    cols = [[lax.dynamic_slice(obs_taper, (local[k] * NBLK, batch_order[j] * NBLK), (NBLK, NBLK)) for j in range(NB)] for k in range(NB)]
    cross = lookup(taper_levels, jnp.stack([jnp.stack(c) for c in cols])).reshape(NB, NB * NBLK * NBLK)
    for k in range(NB):
        dep = lax.dynamic_index_in_dim(obs_depart, local[k], 0, keepdims=False)
        var = lax.dynamic_index_in_dim(obs_var, local[k], 0, keepdims=False)
        lines.append(jnp.concatenate([dep, var, cross[k], jnp.zeros((M - 2 * PIECE - NB * NBLK * NBLK,), F32)]))
    lines = jnp.concatenate([jnp.stack(lines), jnp.zeros((8 - NB, M), F32)])
    payload = jnp.concatenate([pieces[0], lines, pieces[2][24:], pieces[1], pieces[2][:24]])
    kinds = [0] * 32 + [0, 1, 2] + [0] * 5 + [2] * 8 + [1] * 32 + [2] * 24
    kind = jnp.array(kinds, jnp.int32)

    def per_row(flags):
        rows = jnp.where(kind == 0, flags[0], jnp.where(kind == 1, flags[1], flags[2]))
        return rows[:, None]

    payload = spread(payload, owner // YS, "x", XS, per_row)
    payload = spread(payload, owner % YS, "y", YS, per_row)
    one = lax.all_gather(payload[:48], ("z", "c"))
    two = lax.all_gather(payload[48:], ("z", "c"))

    mine = shard * PIECE // B
    weights = []
    for k in range(NB):
        at = batch_order[k] * NBLK
        state_part = lax.dynamic_slice_in_dim(state_taper, at, NBLK, 1)
        obs_part = jnp.concatenate(
            [lax.dynamic_slice(obs_taper, (q * NBLK + mine, at), (1, NBLK)) for q in range(KB)]
        )
        weights.append(jnp.concatenate([state_part, obs_part]))
    weights = lookup(taper_levels, jnp.stack(weights))

    rows = state_anom.shape[0]
    anomaly, mean, obs_now, moved = analysis(
        weights, one, two, state_anom, state_mean.reshape(rows // B, B), obs_anom.reshape(KB * PIECE, M)
    )
    return (
        anomaly,
        mean.reshape(rows),
        obs_now.reshape(obs_anom.shape),
        obs_depart - moved[:, :PIECE],
    )


def solution(mesh):
    fine = Mesh(mesh.devices.reshape(XS, YS, ZS, CS), ("x", "y", "z", "c")) if hasattr(mesh, "devices") else mesh
    region, shard, both = ("x", "y"), ("z", "c"), ("x", "y", "z", "c")
    placed = (
        P(both, None),
        P(both),
        P(region, shard, None),
        P(region, shard),
        P(region, shard),
        P(),
        P(both, None),
        P(region, None),
        P(),
    )
    return jax.shard_map(
        per_device,
        mesh=fine,
        in_specs=placed,
        out_specs=(P(both, None), P(both), P(region, shard, None), P(region, shard)),
        check_vma=False,
    )
```

```python
import jax
import jax.numpy as jnp
from jax import lax
from jax.experimental import pallas as pl
from jax.experimental.pallas import tpu as pltpu
from jax.sharding import Mesh, PartitionSpec as P

M = 256
N = 512
B = 128
NBLK = N // B
NB = 3
KB = 2
XS, YS, ZS, CS = 4, 8, 8, 2
PIECE = 32
WIDE = M + B
HI = lax.Precision.HIGHEST
F32 = jnp.float32


def mm(a, b, ca=1, cb=0):
    return lax.dot_general(a, b, (((ca,), (cb,)), ((), ())), precision=HI, preferred_element_type=F32)


def iota(shape, axis):
    return lax.broadcasted_iota(jnp.int32, shape, axis)


def wide(v):
    return jnp.concatenate([v, v], axis=1)


def split(v):
    hi = v.astype(jnp.bfloat16)
    rest = v - hi.astype(F32)
    mid = rest.astype(jnp.bfloat16)
    return hi, mid, (rest - mid.astype(F32)).astype(jnp.bfloat16)


def factor_block(a_ref, p_ref, w_ref):
    groups = B // 8
    rows = [jnp.broadcast_to(a_ref[s : s + 1, :], (8, 2 * B)) for s in range(8)]
    for g in range(groups):
        j0 = 8 * g
        d = {}
        for s in range(8):
            for t in range(s + 1):
                d[s, t] = jnp.broadcast_to(rows[t][:, j0 + s : j0 + s + 1], (8, B))
        if g < groups - 1:
            ahead = [jnp.broadcast_to(a_ref[j0 + 8 + s : j0 + 9 + s, :], (8, 2 * B)) for s in range(8)]
        low = {}
        for t in range(8):
            inv = lax.rsqrt(d[t, t])
            done = rows[t] * wide(inv)
            for s in range(t + 1, 8):
                low[s, t] = d[s, t] * inv
            for s in range(t + 1, 8):
                for v in range(t + 1, s + 1):
                    d[s, v] = d[s, v] - low[s, t] * low[v, t]
            for s in range(t + 1, 8):
                rows[s] = rows[s] - wide(low[s, t]) * done
            w_ref[j0 + t : j0 + t + 1, :] = done[:1, B:]
            if g < groups - 1:
                p_ref[j0 + t : j0 + t + 1, :] = done[:1, :]
                for s in range(8):
                    ahead[s] = ahead[s] - wide(jnp.broadcast_to(done[:, j0 + 8 + s : j0 + 9 + s], (8, B))) * done
        if g == groups - 1:
            break
        rows = ahead
        lo = j0 + 16
        if lo < B:
            hi, mid, rest = split(p_ref[j0 : j0 + 8, :])
            left = jnp.concatenate([hi, hi, hi, mid, mid, rest])[:, :B]
            right = jnp.concatenate([hi, mid, rest, hi, mid, hi])
            fix = lax.dot_general(left, right, (((0,), (0,)), ((), ())), preferred_element_type=F32)
            a_ref[lo:, :] = a_ref[lo:, :] - fix[lo:, :]

def lower_inverses(ts):
    ri, ci = iota((B, B), 0), iota((B, B), 1)
    xs = [jnp.where(ri == ci, 1.0 / t, 0.0) for t in ts]
    m = 1
    while m < B:
        mask = (ri // (2 * m) == ci // (2 * m)) & ((ri // m) % 2 == 1) & ((ci // m) % 2 == 0)
        mid = [mm(jnp.where(mask, t, 0.0), x) for t, x in zip(ts, xs)]
        xs = [x - mm(x, y) for x, y in zip(xs, mid)]
        m *= 2
    return xs


def analysis_kernel(
    order_ref, levels_ref, stape_ref, otape_ref, mine_ref, one_ref, two_ref, x_ref, mean_ref, obs_ref,
    xo_ref, meano_ref, obso_ref, depo_ref,
    y_ref, d_ref, r_ref, c_ref, s_ref, u_ref, w_ref, a_ref, p_ref, v_ref, g_ref, dm_ref, do_ref,
):
    eye = iota((B, B), 0) == iota((B, B), 1)
    low_mask = iota((B, B), 0) >= iota((B, B), 1)
    piece_eye = iota((PIECE, B), 0) == iota((PIECE, B), 1)
    var_eye = iota((PIECE, B), 0) + PIECE == iota((PIECE, B), 1)
    pairs = NB * NBLK * NBLK
    pair_eye = iota((pairs, B), 0) + 2 * PIECE == iota((pairs, B), 1)

    def column(line, mask):
        col = jnp.sum(jnp.where(mask, line, 0.0), axis=1, keepdims=True)
        return jnp.broadcast_to(col, mask.shape)

    def unpack(s, carry):
        at = pl.multiple_of(s * PIECE, PIECE)
        y_ref[0, pl.ds(at, 32), :] = one_ref[s, 0:32, :]
        y_ref[1, pl.ds(at, 32), :] = two_ref[s, 0:32, :]
        y_ref[2, pl.ds(at, 24), :] = two_ref[s, 32:56, :]
        y_ref[2, pl.ds(at + 24, 8), :] = one_ref[s, 40:48, :]
        for k in range(NB):
            line = one_ref[s, 32 + k : 33 + k, :B]
            d_ref[k, pl.ds(at, PIECE), :] = column(line, piece_eye)
            r_ref[k, pl.ds(at, PIECE), :] = column(line, var_eye)
        return carry

    lax.fori_loop(0, ZS * CS, unpack, 0)
    for k in range(NB):
        c_ref[k * pairs : k * pairs + pairs, :] = column(one_ref[0, 32 + k : 33 + k, :B], pair_eye)
    xo_ref[...] = x_ref[...]
    obso_ref[...] = obs_ref[...]
    dm_ref[...] = jnp.zeros_like(dm_ref)
    do_ref[...] = jnp.zeros_like(do_ref)

    def batch_step(k, outer):
        s_ref[:, :N] = mm(y_ref[k], y_ref[k], 1, 1) * (1.0 / (M - 1))
        s_ref[:, N:] = d_ref[k]
        for b in range(NBLK):
            sl = slice(b * B, b * B + B)
            s_ref[sl, sl] = s_ref[sl, sl] + jnp.where(eye, r_ref[k, sl, :], 0.0)

        def block_step(b, carry):
            at = pl.multiple_of(b * B, B)
            a_ref[:, :B] = s_ref[pl.ds(at, B), pl.ds(at, B)]
            a_ref[:, B:] = jnp.where(eye, 1.0, 0.0)
            factor_block(a_ref, p_ref, w_ref.at[b])
            inv = w_ref[b]
            row = mm(inv, s_ref[pl.ds(at, B), :])
            u_ref[pl.ds(at, B), :] = row
            for c in range(NBLK - 1):
                @pl.when(b == c)
                def _():
                    lo = (c + 1) * B
                    q = mm(inv, u_ref[lo - B : lo, lo:], 0, 0)
                    s_ref[lo:, lo:] = s_ref[lo:, lo:] - mm(s_ref[lo:, lo - B : lo], q)
            return carry

        lax.fori_loop(0, NBLK, block_step, 0)

        shifted = []
        for b in range(NBLK):
            sl = slice(b * B, b * B + B)
            low = jnp.where(low_mask, jnp.transpose(u_ref[sl, sl]), 0.0)
            shifted.append(low + jnp.where(eye, jnp.sqrt(r_ref[k, sl, :]), 0.0))
        tinv = lower_inverses(shifted)

        v_ref[:, :M] = y_ref[k]
        v_ref[:, M:] = u_ref[:, N:]
        for b in range(NBLK):
            sl = slice(b * B, b * B + B)
            hi = (b + 1) * B
            v_ref[sl, :M] = mm(tinv[b], v_ref[sl, :M])
            if b < NBLK - 1:
                v_ref[hi:, :M] = v_ref[hi:, :M] - mm(u_ref[sl, hi:N], v_ref[sl, :M], 0, 0)
        for b in range(NBLK - 1, -1, -1):
            sl = slice(b * B, b * B + B)
            hi = (b + 1) * B
            rhs = v_ref[sl, :]
            if b < NBLK - 1:
                rhs = rhs - mm(u_ref[sl, hi:N], v_ref[hi:, :])
            v_ref[sl, :] = mm(w_ref[b], rhs, 0, 0)
        for b in range(NBLK):
            sl = slice(b * B, b * B + B)
            g_ref[b] = mm(y_ref[k, sl, :], v_ref[sl, :], 0, 0) * (1.0 / (M - 1))

        def gain(weight):
            total = weight(0) * g_ref[0]
            for j in range(1, NBLK):
                total = total + weight(j) * g_ref[j]
            return total

        def cross_step(n, carry):
            later, i = n // NBLK, n % NBLK
            at = pl.multiple_of(i * B, B)

            def weight(j):
                line = c_ref[pl.ds(later * pairs + k * (NBLK * NBLK) + i * NBLK + j, 1), :]
                return jnp.concatenate([line] * (WIDE // B), axis=1)

            delta = mm(y_ref[later, pl.ds(at, B), :], gain(weight))
            y_ref[later, pl.ds(at, B), :] = y_ref[later, pl.ds(at, B), :] - delta[:, :M]
            d_ref[later, pl.ds(at, B), :] = d_ref[later, pl.ds(at, B), :] - delta[:, M:]
            return carry

        lax.fori_loop((k + 1) * NBLK, NB * NBLK, cross_step, 0)
        first = order_ref[k] * NBLK

        def state_step(i, carry):
            at = pl.multiple_of(i * B, B)
            rows = xo_ref[pl.ds(at, B), :]
            delta = mm(rows, gain(lambda j: levels_ref[stape_ref[i, first + j]]))
            xo_ref[pl.ds(at, B), :] = rows - delta[:, :M]
            dm_ref[pl.ds(at, B), :] = dm_ref[pl.ds(at, B), :] + delta[:, M:]
            return carry

        lax.fori_loop(0, x_ref.shape[0] // B, state_step, 0)
        for q in range(KB):
            sl = slice(q * PIECE, q * PIECE + PIECE)
            rows = obso_ref[sl, :]
            delta = mm(rows, gain(lambda j: levels_ref[otape_ref[q * NBLK + mine_ref[0], first + j]]))
            obso_ref[sl, :] = rows - delta[:, :M]
            do_ref[sl, :] = do_ref[sl, :] + delta[:, M:]
        return outer

    lax.fori_loop(0, NB, batch_step, 0)

    for i in range(x_ref.shape[0] // B):
        sl = slice(i * B, i * B + B)
        add = jnp.sum(jnp.where(eye, dm_ref[sl, :], 0.0), axis=0, keepdims=True)
        meano_ref[i : i + 1, :] = mean_ref[i : i + 1, :] + add
    for q in range(KB):
        sl = slice(q * PIECE, q * PIECE + PIECE)
        sub = jnp.sum(jnp.where(piece_eye, do_ref[sl, :], 0.0), axis=0, keepdims=True)
        depo_ref[q : q + 1, :] = sub


def analysis(order, levels, stape, otape, mine, one, two, x, mean, obs):
    shape = lambda *dims: jax.ShapeDtypeStruct(dims, F32)
    scratch = lambda *dims: pltpu.VMEM(dims, F32)
    vmem = pl.BlockSpec(memory_space=pltpu.VMEM)
    rows = x.shape[0]
    return pl.pallas_call(
        analysis_kernel,
        out_shape=[shape(rows, M), shape(rows // B, B), shape(KB * PIECE, M), shape(KB, B)],
        in_specs=[pl.BlockSpec(memory_space=pltpu.SMEM)] * 5 + [vmem] * 5,
        out_specs=[vmem] * 4,
        scratch_shapes=[
            scratch(NB, N, M),
            scratch(NB, N, B),
            scratch(NB, N, B),
            scratch(NB * NB * NBLK * NBLK, B),
            scratch(N, N + B),
            scratch(N, N + B),
            scratch(NBLK, B, B),
            scratch(B, 2 * B),
            scratch(B, 2 * B),
            scratch(N, WIDE),
            scratch(NBLK, M, WIDE),
            scratch(rows, B),
            scratch(KB * PIECE, B),
        ],
        name="analysis",
    )(order, levels, stape, otape, mine, one, two, x, mean, obs)


ROWS = 104


def prepare_kernel(order_ref, levels_ref, otape_ref, obs_ref, dep_ref, var_ref, out_ref):
    local = [order_ref[k] % KB for k in range(NB)]
    out_ref[0:32, :] = obs_ref[local[0]]
    out_ref[48:80, :] = obs_ref[local[1]]
    out_ref[80:104, :] = obs_ref[local[2], 0:24, :]
    out_ref[40:48, :] = obs_ref[local[2], 24:32, :]
    out_ref[32:40, :] = jnp.zeros((8, M), F32)
    lane = iota((1, B), 1)
    for k in range(NB):
        line = jnp.zeros((1, B), F32)
        for b in range(NB):
            for i in range(NBLK):
                for j in range(NBLK):
                    weight = levels_ref[otape_ref[local[k] * NBLK + i, order_ref[b] * NBLK + j]]
                    line = jnp.where(lane == 2 * PIECE + (b * NBLK + i) * NBLK + j, weight, line)
        out_ref[32 + k : 33 + k, :B] = line
        for q in range(KB):
            @pl.when(local[k] == q)
            def _():
                out_ref[32 + k : 33 + k, 0:PIECE] = dep_ref[q : q + 1, :]
                out_ref[32 + k : 33 + k, PIECE : 2 * PIECE] = var_ref[q : q + 1, :]


def prepare(order, levels, otape, obs, dep, var):
    vmem = pl.BlockSpec(memory_space=pltpu.VMEM)
    return pl.pallas_call(
        prepare_kernel,
        out_shape=jax.ShapeDtypeStruct((ROWS, M), F32),
        in_specs=[pl.BlockSpec(memory_space=pltpu.SMEM)] * 3 + [vmem] * 3,
        out_specs=vmem,
        name="prepare",
    )(order, levels, otape, obs, dep, var)


def spread(block, roots, axis, size):
    place = lax.axis_index(axis)
    away = [(place - roots[k] + size) % size for k in range(NB)]
    row = iota(block.shape, 0)
    second = (row == 33) | ((row >= 48) & (row < 80))
    third = (row == 34) | ((row >= 40) & (row < 48)) | (row >= 80)
    far = jnp.where(second, away[1], jnp.where(third, away[2], away[0]))
    step = size // 2
    while step:
        moved = lax.ppermute(block, axis, [(i, (i + step) % size) for i in range(size)])
        block = jnp.where(far % (2 * step) == 0, block, moved)
        step //= 2
    return block


def per_device(state_anom, state_mean, obs_anom, obs_depart, obs_var, taper_levels, state_taper, obs_taper, batch_order):
    shard = lax.axis_index("z") * CS + lax.axis_index("c")
    owner = batch_order // KB
    payload = prepare(batch_order, taper_levels, obs_taper, obs_anom, obs_depart, obs_var)
    payload = spread(payload, owner // YS, "x", XS)
    payload = spread(payload, owner % YS, "y", YS)
    one = lax.all_gather(payload[:48], ("z", "c"))
    two = lax.all_gather(payload[48:], ("z", "c"))
    mine = (shard * PIECE // B).astype(jnp.int32).reshape(1)
    rows = state_anom.shape[0]
    anomaly, mean, obs_now, moved = analysis(
        batch_order, taper_levels, state_taper, obs_taper, mine, one, two,
        state_anom, state_mean.reshape(rows // B, B), obs_anom.reshape(KB * PIECE, M),
    )
    return (
        anomaly,
        mean.reshape(rows),
        obs_now.reshape(obs_anom.shape),
        obs_depart - moved[:, :PIECE],
    )


def solution(mesh):
    fine = Mesh(mesh.devices.reshape(XS, YS, ZS, CS), ("x", "y", "z", "c")) if hasattr(mesh, "devices") else mesh
    region, shard, both = ("x", "y"), ("z", "c"), ("x", "y", "z", "c")
    placed = (
        P(both, None),
        P(both),
        P(region, shard, None),
        P(region, shard),
        P(region, shard),
        P(),
        P(both, None),
        P(region, None),
        P(),
    )
    return jax.shard_map(
        per_device,
        mesh=fine,
        in_specs=placed,
        out_specs=(P(both, None), P(both), P(region, shard, None), P(region, shard)),
        check_vma=False,
    )
```

```python
import jax
import jax.numpy as jnp
from jax import lax
from jax.experimental import pallas as pl
from jax.experimental.pallas import tpu as pltpu
from jax.sharding import Mesh, PartitionSpec as P

M = 256
N = 512
B = 128
NBLK = N // B
NB = 3
KB = 2
XS, YS, ZS, CS = 4, 8, 8, 2
PIECE = 32
WIDE = M + B
HI = lax.Precision.HIGHEST
F32 = jnp.float32


def mm(a, b, ca=1, cb=0):
    return lax.dot_general(a, b, (((ca,), (cb,)), ((), ())), precision=HI, preferred_element_type=F32)


def halves(v):
    hi = v.astype(jnp.bfloat16)
    return hi, (v - hi.astype(F32)).astype(jnp.bfloat16)


def mm3(a, b, ca=1, cb=0):
    dot = lambda p, q: lax.dot_general(p, q, (((ca,), (cb,)), ((), ())), preferred_element_type=F32)
    (ah, al), (bh, bl) = halves(a), halves(b)
    return dot(ah, bh) + (dot(ah, bl) + dot(al, bh))


def iota(shape, axis):
    return lax.broadcasted_iota(jnp.int32, shape, axis)


def wide(v):
    return jnp.concatenate([v, v], axis=1)


def split(v):
    hi = v.astype(jnp.bfloat16)
    rest = v - hi.astype(F32)
    mid = rest.astype(jnp.bfloat16)
    return hi, mid, (rest - mid.astype(F32)).astype(jnp.bfloat16)


def factor_block(a_ref, p_ref, w_ref, root_ref, base_ref, hooks):
    groups = B // 8
    lane = iota((8, B), 1)
    rows = [jnp.broadcast_to(a_ref[s : s + 1, :], (8, 2 * B)) for s in range(8)]
    for g in range(groups):
        j0 = 8 * g
        d = {}
        for s in range(8):
            for t in range(s + 1):
                d[s, t] = jnp.broadcast_to(rows[t][:, j0 + s : j0 + s + 1], (8, B))
        if g < groups - 1:
            ahead = [jnp.broadcast_to(a_ref[j0 + 8 + s : j0 + 9 + s, :], (8, 2 * B)) for s in range(8)]
        low, diag = {}, []
        for t in range(8):
            inv = lax.rsqrt(d[t, t])
            diag.append(d[t, t] * inv)
            done = rows[t] * wide(inv)
            for s in range(t + 1, 8):
                low[s, t] = d[s, t] * inv
            for s in range(t + 1, 8):
                for v in range(t + 1, s + 1):
                    d[s, v] = d[s, v] - low[s, t] * low[v, t]
            for s in range(t + 1, 8):
                rows[s] = rows[s] - wide(low[s, t]) * done
            w_ref[j0 + t : j0 + t + 1, :] = done[:1, B:]
            if g < groups - 1:
                p_ref[j0 + t : j0 + t + 1, :] = done[:1, :]
                for s in range(8):
                    ahead[s] = ahead[s] - wide(jnp.broadcast_to(done[:, j0 + 8 + s : j0 + 9 + s], (8, B))) * done
        small = []
        for s in range(8):
            row = jnp.where(lane == j0 + s, 1.0, 0.0)
            for t in range(s):
                row = row - low[s, t] * small[t]
            shift = jnp.broadcast_to(root_ref[j0 + s : j0 + s + 1, :], (8, B))
            small.append(row * (1.0 / (diag[s] + shift)))
            base_ref[j0 + s : j0 + s + 1, :] = small[s][:1, :]
        if hooks.get(g):
            hooks[g]()
        if g == groups - 1:
            break
        rows = ahead
        lo = j0 + 16
        if lo < B:
            hi, mid, rest = split(p_ref[j0 : j0 + 8, :])
            left = jnp.concatenate([hi, hi, hi, mid, mid, rest])[:, :B]
            right = jnp.concatenate([hi, mid, rest, hi, mid, hi])
            fix = lax.dot_general(left, right, (((0,), (0,)), ((), ())), preferred_element_type=F32)
            a_ref[lo:, :] = a_ref[lo:, :] - fix[lo:, :]

def doubling_steps(u, low_ref, x_ref, mid_ref):
    ri, ci = iota((B, B), 0), iota((B, B), 1)

    def first():
        low_ref[...] = jnp.transpose(u())

    def half(m):
        mask = (ri // (2 * m) == ci // (2 * m)) & ((ri // m) % 2 == 1) & ((ci // m) % 2 == 0)
        mid_ref[...] = mm(jnp.where(mask, low_ref[...], 0.0), x_ref[...])

    def full():
        x_ref[...] = x_ref[...] - mm(x_ref[...], mid_ref[...])

    steps = [first]
    for m in (8, 16, 32, 64):
        steps += [lambda m=m: half(m), full]
    return steps


BASE = NBLK


def analysis_kernel(
    order_ref, levels_ref, stape_ref, otape_ref, mine_ref, one_ref, two_ref, x_ref, mean_ref, obs_ref,
    xo_ref, meano_ref, obso_ref, depo_ref,
    y_ref, d_ref, r_ref, c_ref, s_ref, u_ref, w_ref, a_ref, p_ref, v_ref, g_ref, dm_ref, do_ref, e_ref, x8_ref, low_ref, mid_ref, qr_ref,
):
    eye = iota((B, B), 0) == iota((B, B), 1)
    piece_eye = iota((PIECE, B), 0) == iota((PIECE, B), 1)
    var_eye = iota((PIECE, B), 0) + PIECE == iota((PIECE, B), 1)
    pairs = NB * NBLK * NBLK
    pair_eye = iota((pairs, B), 0) + 2 * PIECE == iota((pairs, B), 1)

    def column(line, mask):
        col = jnp.sum(jnp.where(mask, line, 0.0), axis=1, keepdims=True)
        return jnp.broadcast_to(col, mask.shape)

    def unpack(s, carry):
        at = pl.multiple_of(s * PIECE, PIECE)
        y_ref[0, pl.ds(at, 32), :] = one_ref[s, 0:32, :]
        y_ref[1, pl.ds(at, 32), :] = two_ref[s, 0:32, :]
        y_ref[2, pl.ds(at, 24), :] = two_ref[s, 32:56, :]
        y_ref[2, pl.ds(at + 24, 8), :] = one_ref[s, 40:48, :]
        for k in range(NB):
            line = one_ref[s, 32 + k : 33 + k, :B]
            d_ref[k, pl.ds(at, PIECE), :] = column(line, piece_eye)
            var = column(line, var_eye)
            r_ref[k, pl.ds(at, PIECE), :] = var
            e_ref[k, pl.ds(at, PIECE), :] = jnp.sqrt(var)
        return carry

    lax.fori_loop(0, ZS * CS, unpack, 0)
    for k in range(NB):
        c_ref[k * pairs : k * pairs + pairs, :] = column(one_ref[0, 32 + k : 33 + k, :B], pair_eye)
    xo_ref[...] = x_ref[...]
    obso_ref[...] = obs_ref[...]
    dm_ref[...] = jnp.zeros_like(dm_ref)
    do_ref[...] = jnp.zeros_like(do_ref)

    def batch_step(k, outer):
        s_ref[:, :N] = mm(y_ref[k], y_ref[k], 1, 1) * (1.0 / (M - 1))
        s_ref[:, N:] = d_ref[k]
        for b in range(NBLK):
            sl = slice(b * B, b * B + B)
            s_ref[sl, sl] = s_ref[sl, sl] + jnp.where(eye, r_ref[k, sl, :], 0.0)

        def block_step(b, carry):
            at = pl.multiple_of(b * B, B)
            a_ref[:, :B] = s_ref[pl.ds(at, B), pl.ds(at, B)]
            a_ref[:, B:] = jnp.where(eye, 1.0, 0.0)
            last = jnp.maximum(b - 1, 0)
            seen = pl.multiple_of(last * B, B)
            steps = doubling_steps(
                lambda: u_ref[pl.ds(seen, B), pl.ds(seen, B)], low_ref, x8_ref.at[last], mid_ref
            )
            hooks = {g + 1: step for g, step in enumerate(steps)}
            factor_block(a_ref, p_ref, w_ref.at[b], e_ref.at[k, pl.ds(at, B)], x8_ref.at[BASE], hooks)
            x8_ref[b] = x8_ref[BASE]
            inv = w_ref[b]
            row = mm(inv, s_ref[pl.ds(at, B), :])
            u_ref[pl.ds(at, B), :] = row
            for c in range(NBLK - 1):
                @pl.when(b == c)
                def _():
                    lo = (c + 1) * B
                    q = mm(inv, u_ref[lo - B : lo, lo:], 0, 0)
                    s_ref[lo:, lo:] = s_ref[lo:, lo:] - mm(s_ref[lo:, lo - B : lo], q)
            return carry

        lax.fori_loop(0, NBLK, block_step, 0)

        tail = (NBLK - 1) * B
        for step in doubling_steps(
            lambda: u_ref[tail : tail + B, tail : tail + B], low_ref, x8_ref.at[NBLK - 1], mid_ref
        ):
            step()

        v_ref[:, :M] = y_ref[k]
        v_ref[:, M:] = u_ref[:, N:]
        for b in range(NBLK):
            sl = slice(b * B, b * B + B)
            hi = (b + 1) * B
            v_ref[sl, :M] = mm(x8_ref[b], v_ref[sl, :M])
            if b < NBLK - 1:
                v_ref[hi:, :M] = v_ref[hi:, :M] - mm(u_ref[sl, hi:N], v_ref[sl, :M], 0, 0)
        for b in range(NBLK - 1, -1, -1):
            sl = slice(b * B, b * B + B)
            hi = (b + 1) * B
            rhs = v_ref[sl, :]
            if b < NBLK - 1:
                rhs = rhs - mm(u_ref[sl, hi:N], v_ref[hi:, :])
            v_ref[sl, :] = mm(w_ref[b], rhs, 0, 0)
        for b in range(NBLK):
            sl = slice(b * B, b * B + B)
            g_ref[b] = mm3(y_ref[k, sl, :], v_ref[sl, :M], 0, 0) * (1.0 / (M - 1))
            line = jnp.sum(y_ref[k, sl, :] * wide(v_ref[sl, M:]), axis=0, keepdims=True)
            qr_ref[b : b + 1, :] = line * (1.0 / (M - 1))

        def update(rows, weight):
            mat = weight(0) * g_ref[0]
            line = weight(0) * qr_ref[0:1, :]
            for j in range(1, NBLK):
                mat = mat + weight(j) * g_ref[j]
                line = line + weight(j) * qr_ref[j : j + 1, :]
            move = jnp.sum(rows * line, axis=1, keepdims=True)
            return mm3(rows, mat), jnp.broadcast_to(move, (rows.shape[0], B))

        def cross_step(n, carry):
            later, i = n // NBLK, n % NBLK
            at = pl.multiple_of(i * B, B)

            def weight(j):
                line = c_ref[pl.ds(later * pairs + k * (NBLK * NBLK) + i * NBLK + j, 1), :]
                return jnp.concatenate([line] * (M // B), axis=1)

            rows = y_ref[later, pl.ds(at, B), :]
            delta, move = update(rows, weight)
            y_ref[later, pl.ds(at, B), :] = rows - delta
            d_ref[later, pl.ds(at, B), :] = d_ref[later, pl.ds(at, B), :] - move
            return carry

        lax.fori_loop((k + 1) * NBLK, NB * NBLK, cross_step, 0)
        first = order_ref[k] * NBLK

        def state_step(i, carry):
            at = pl.multiple_of(i * B, B)
            rows = xo_ref[pl.ds(at, B), :]
            delta, move = update(rows, lambda j: levels_ref[stape_ref[i, first + j]])
            xo_ref[pl.ds(at, B), :] = rows - delta
            dm_ref[pl.ds(at, B), :] = dm_ref[pl.ds(at, B), :] + move
            return carry

        lax.fori_loop(0, x_ref.shape[0] // B, state_step, 0)
        for q in range(KB):
            sl = slice(q * PIECE, q * PIECE + PIECE)
            rows = obso_ref[sl, :]
            delta, move = update(rows, lambda j: levels_ref[otape_ref[q * NBLK + mine_ref[0], first + j]])
            obso_ref[sl, :] = rows - delta
            do_ref[sl, :] = do_ref[sl, :] + move
        return outer

    lax.fori_loop(0, NB, batch_step, 0)

    for i in range(x_ref.shape[0] // B):
        sl = slice(i * B, i * B + B)
        add = jnp.sum(jnp.where(eye, dm_ref[sl, :], 0.0), axis=0, keepdims=True)
        meano_ref[i : i + 1, :] = mean_ref[i : i + 1, :] + add
    for q in range(KB):
        sl = slice(q * PIECE, q * PIECE + PIECE)
        sub = jnp.sum(jnp.where(piece_eye, do_ref[sl, :], 0.0), axis=0, keepdims=True)
        depo_ref[q : q + 1, :] = sub


def analysis(order, levels, stape, otape, mine, one, two, x, mean, obs):
    shape = lambda *dims: jax.ShapeDtypeStruct(dims, F32)
    scratch = lambda *dims: pltpu.VMEM(dims, F32)
    vmem = pl.BlockSpec(memory_space=pltpu.VMEM)
    rows = x.shape[0]
    return pl.pallas_call(
        analysis_kernel,
        out_shape=[shape(rows, M), shape(rows // B, B), shape(KB * PIECE, M), shape(KB, B)],
        in_specs=[pl.BlockSpec(memory_space=pltpu.SMEM)] * 5 + [vmem] * 5,
        out_specs=[vmem] * 4,
        scratch_shapes=[
            scratch(NB, N, M),
            scratch(NB, N, B),
            scratch(NB, N, B),
            scratch(NB * NB * NBLK * NBLK, B),
            scratch(N, N + B),
            scratch(N, N + B),
            scratch(NBLK, B, B),
            scratch(B, 2 * B),
            scratch(B, 2 * B),
            scratch(N, WIDE),
            scratch(NBLK, M, M),
            scratch(rows, B),
            scratch(KB * PIECE, B),
            scratch(NB, N, B),
            scratch(NBLK + 1, B, B),
            scratch(B, B),
            scratch(B, B),
            scratch(8, M),
        ],
        name="analysis",
    )(order, levels, stape, otape, mine, one, two, x, mean, obs)


ROWS = 104


def prepare_kernel(order_ref, levels_ref, otape_ref, obs_ref, dep_ref, var_ref, out_ref):
    local = [order_ref[k] % KB for k in range(NB)]
    out_ref[0:32, :] = obs_ref[local[0]]
    out_ref[48:80, :] = obs_ref[local[1]]
    out_ref[80:104, :] = obs_ref[local[2], 0:24, :]
    out_ref[40:48, :] = obs_ref[local[2], 24:32, :]
    out_ref[32:40, :] = jnp.zeros((8, M), F32)
    lane = iota((1, B), 1)
    for k in range(NB):
        line = jnp.zeros((1, B), F32)
        for b in range(NB):
            for i in range(NBLK):
                for j in range(NBLK):
                    weight = levels_ref[otape_ref[local[k] * NBLK + i, order_ref[b] * NBLK + j]]
                    line = jnp.where(lane == 2 * PIECE + (b * NBLK + i) * NBLK + j, weight, line)
        out_ref[32 + k : 33 + k, :B] = line
        for q in range(KB):
            @pl.when(local[k] == q)
            def _():
                out_ref[32 + k : 33 + k, 0:PIECE] = dep_ref[q : q + 1, :]
                out_ref[32 + k : 33 + k, PIECE : 2 * PIECE] = var_ref[q : q + 1, :]


def prepare(order, levels, otape, obs, dep, var):
    vmem = pl.BlockSpec(memory_space=pltpu.VMEM)
    return pl.pallas_call(
        prepare_kernel,
        out_shape=jax.ShapeDtypeStruct((ROWS, M), F32),
        in_specs=[pl.BlockSpec(memory_space=pltpu.SMEM)] * 3 + [vmem] * 3,
        out_specs=vmem,
        name="prepare",
    )(order, levels, otape, obs, dep, var)


def spread(block, roots, axis, size):
    place = lax.axis_index(axis)
    away = [(place - roots[k] + size) % size for k in range(NB)]
    row = iota(block.shape, 0)
    second = (row == 33) | ((row >= 48) & (row < 80))
    third = (row == 34) | ((row >= 40) & (row < 48)) | (row >= 80)
    far = jnp.where(second, away[1], jnp.where(third, away[2], away[0]))
    step = size
    while step > 1:
        fan = 2 if step == 8 else 4
        step //= fan
        moved = {
            n: lax.ppermute(block, axis, [(i, (i + n * step) % size) for i in range(size)]) for n in range(1, fan)
        }
        part = far % (fan * step)
        for n in moved:
            block = jnp.where(part // step == n, moved[n], block)
    return block


def per_device(state_anom, state_mean, obs_anom, obs_depart, obs_var, taper_levels, state_taper, obs_taper, batch_order):
    shard = lax.axis_index("z") * CS + lax.axis_index("c")
    owner = batch_order // KB
    payload = prepare(batch_order, taper_levels, obs_taper, obs_anom, obs_depart, obs_var)
    payload = spread(payload, owner // YS, "x", XS)
    payload = spread(payload, owner % YS, "y", YS)
    one = lax.all_gather(payload[:48], ("z", "c"))
    two = lax.all_gather(payload[48:], ("z", "c"))
    mine = (shard * PIECE // B).astype(jnp.int32).reshape(1)
    rows = state_anom.shape[0]
    anomaly, mean, obs_now, moved = analysis(
        batch_order, taper_levels, state_taper, obs_taper, mine, one, two,
        state_anom, state_mean.reshape(rows // B, B), obs_anom.reshape(KB * PIECE, M),
    )
    return (
        anomaly,
        mean.reshape(rows),
        obs_now.reshape(obs_anom.shape),
        obs_depart - moved[:, :PIECE],
    )


def solution(mesh):
    fine = Mesh(mesh.devices.reshape(XS, YS, ZS, CS), ("x", "y", "z", "c")) if hasattr(mesh, "devices") else mesh
    region, shard, both = ("x", "y"), ("z", "c"), ("x", "y", "z", "c")
    placed = (
        P(both, None),
        P(both),
        P(region, shard, None),
        P(region, shard),
        P(region, shard),
        P(),
        P(both, None),
        P(region, None),
        P(),
    )
    return jax.shard_map(
        per_device,
        mesh=fine,
        in_specs=placed,
        out_specs=(P(both, None), P(both), P(region, shard, None), P(region, shard)),
        check_vma=False,
    )
```

```python
import jax
import jax.numpy as jnp
from jax import lax
from jax.experimental import pallas as pl
from jax.experimental.pallas import tpu as pltpu
from jax.sharding import Mesh, PartitionSpec as P

M = 256
N = 512
B = 128
NBLK = N // B
NB = 3
KB = 2
XS, YS, ZS, CS = 4, 8, 8, 2
PIECE = 32
WIDE = M + B
HI = lax.Precision.HIGHEST
F32 = jnp.float32


def mm(a, b, ca=1, cb=0):
    return lax.dot_general(a, b, (((ca,), (cb,)), ((), ())), precision=HI, preferred_element_type=F32)


def halves(v):
    hi = v.astype(jnp.bfloat16)
    return hi, (v - hi.astype(F32)).astype(jnp.bfloat16)


def mm3(a, b, ca=1, cb=0):
    dot = lambda p, q: lax.dot_general(p, q, (((ca,), (cb,)), ((), ())), preferred_element_type=F32)
    (ah, al), (bh, bl) = halves(a), halves(b)
    return dot(ah, bh) + (dot(ah, bl) + dot(al, bh))


def iota(shape, axis):
    return lax.broadcasted_iota(jnp.int32, shape, axis)


def wide(v):
    return jnp.concatenate([v, v], axis=1)


def split(v):
    hi = v.astype(jnp.bfloat16)
    rest = v - hi.astype(F32)
    mid = rest.astype(jnp.bfloat16)
    return hi, mid, (rest - mid.astype(F32)).astype(jnp.bfloat16)


def factor_block(a_ref, p_ref, w_ref, root_ref, base_ref, n_ref, c_ref, hooks):
    groups = B // 8
    lane = iota((8, B), 1)
    rows = [jnp.broadcast_to(a_ref[s : s + 1, :], (8, 2 * B)) for s in range(8)]
    corner = a_ref[0:8, :B]
    for g in range(groups):
        j0 = 8 * g
        slot = 64 * (g % 2)
        for t in range(8):
            c_ref[slot + 8 * t : slot + 8 * t + 8, :] = jnp.broadcast_to(corner[:, j0 + t : j0 + t + 1], (8, B))
        d = {}
        for s in range(8):
            for t in range(s + 1):
                at = slot + 8 * t + s
                d[s, t] = jnp.broadcast_to(c_ref[at : at + 1, :], (8, B))
        low, diag = {}, []
        for t in range(8):
            inv = lax.rsqrt(d[t, t])
            diag.append(d[t, t] * inv)
            done = rows[t] * wide(inv)
            for s in range(t + 1, 8):
                low[s, t] = d[s, t] * inv
            for s in range(t + 1, 8):
                for v in range(t + 1, s + 1):
                    d[s, v] = d[s, v] - low[s, t] * low[v, t]
            for s in range(t + 1, 8):
                rows[s] = rows[s] - wide(low[s, t]) * done
            w_ref[j0 + t : j0 + t + 1, :] = done[:1, B:]
            if g < groups - 1:
                p_ref[j0 + t : j0 + t + 1, :] = done[:1, :]
        if g < groups - 1:
            panel = p_ref[j0 : j0 + 8, :]
            ahead = []
            turn = 8 * (g % 2)
            for s in range(8):
                j1 = j0 + 8 + s
                fix = wide(jnp.broadcast_to(panel[:, j1 : j1 + 1], (8, B))) * panel
                for step in (4, 2, 1):
                    fix = fix + pltpu.roll(fix, step, 0)
                ahead.append(jnp.broadcast_to(a_ref[j1 : j1 + 1, :], (8, 2 * B)) - fix)
                n_ref[turn + s : turn + s + 1, :] = ahead[s][:1, :B]
            corner = n_ref[turn : turn + 8, :]
        small = []
        for s in range(8):
            row = jnp.where(lane == j0 + s, 1.0, 0.0)
            for t in range(s):
                row = row - low[s, t] * small[t]
            shift = jnp.broadcast_to(root_ref[j0 + s : j0 + s + 1, :], (8, B))
            small.append(row * (1.0 / (diag[s] + shift)))
            base_ref[j0 + s : j0 + s + 1, :] = small[s][:1, :]
        if hooks.get(g):
            hooks[g]()
        if g == groups - 1:
            break
        rows = ahead
        lo = j0 + 16
        if lo < B:
            hi, mid, rest = split(p_ref[j0 : j0 + 8, :])
            left = jnp.concatenate([hi, hi, hi, mid, mid, rest])[:, :B]
            right = jnp.concatenate([hi, mid, rest, hi, mid, hi])
            fix = lax.dot_general(left, right, (((0,), (0,)), ((), ())), preferred_element_type=F32)
            a_ref[lo:, :] = a_ref[lo:, :] - fix[lo:, :]

def doubling_steps(u, low_ref, x_ref, mid_ref):
    ri, ci = iota((B, B), 0), iota((B, B), 1)

    def first():
        low_ref[...] = jnp.transpose(u())

    def half(m):
        mask = (ri // (2 * m) == ci // (2 * m)) & ((ri // m) % 2 == 1) & ((ci // m) % 2 == 0)
        mid_ref[...] = mm(jnp.where(mask, low_ref[...], 0.0), x_ref[...])

    def full():
        x_ref[...] = x_ref[...] - mm(x_ref[...], mid_ref[...])

    steps = [first]
    for m in (8, 16, 32, 64):
        steps += [lambda m=m: half(m), full]
    return steps


def forward_steps(cols, y, v_ref, out_ref, x_ref, part_ref, first_row):
    def above():
        factor = jnp.where(iota((N, B), 0) < first_row, cols(), 0.0)
        part_ref[...] = y() - mm(factor, v_ref[:, :M], 0, 0)

    def solve():
        out_ref[...] = mm(x_ref[...], part_ref[...])

    return [above, solve]


BASE = NBLK


def analysis_kernel(
    order_ref, levels_ref, stape_ref, otape_ref, mine_ref, one_ref, two_ref, x_ref, mean_ref, obs_ref,
    xo_ref, meano_ref, obso_ref, depo_ref,
    y_ref, d_ref, r_ref, c_ref, s_ref, u_ref, w_ref, a_ref, p_ref, v_ref, g_ref, dm_ref, do_ref, e_ref, x8_ref, low_ref, mid_ref, qr_ref, n_ref, k_ref, q_ref, part_ref, z_ref,
):
    eye = iota((B, B), 0) == iota((B, B), 1)
    piece_eye = iota((PIECE, B), 0) == iota((PIECE, B), 1)
    var_eye = iota((PIECE, B), 0) + PIECE == iota((PIECE, B), 1)
    pairs = NB * NBLK * NBLK
    pair_eye = iota((pairs, B), 0) + 2 * PIECE == iota((pairs, B), 1)

    def column(line, mask):
        col = jnp.sum(jnp.where(mask, line, 0.0), axis=1, keepdims=True)
        return jnp.broadcast_to(col, mask.shape)

    def unpack(s, carry):
        at = pl.multiple_of(s * PIECE, PIECE)
        y_ref[0, pl.ds(at, 32), :] = one_ref[s, 0:32, :]
        y_ref[1, pl.ds(at, 32), :] = two_ref[s, 0:32, :]
        y_ref[2, pl.ds(at, 24), :] = two_ref[s, 32:56, :]
        y_ref[2, pl.ds(at + 24, 8), :] = one_ref[s, 40:48, :]
        for k in range(NB):
            line = one_ref[s, 32 + k : 33 + k, :B]
            d_ref[k, pl.ds(at, PIECE), :] = column(line, piece_eye)
            var = column(line, var_eye)
            r_ref[k, pl.ds(at, PIECE), :] = var
            e_ref[k, pl.ds(at, PIECE), :] = jnp.sqrt(var)
        return carry

    lax.fori_loop(0, ZS * CS, unpack, 0)
    for k in range(NB):
        c_ref[k * pairs : k * pairs + pairs, :] = column(one_ref[0, 32 + k : 33 + k, :B], pair_eye)
    xo_ref[...] = x_ref[...]
    obso_ref[...] = obs_ref[...]
    dm_ref[...] = jnp.zeros_like(dm_ref)
    do_ref[...] = jnp.zeros_like(do_ref)
    for ref in (u_ref, x8_ref, v_ref, g_ref, qr_ref):
        ref[...] = jnp.zeros_like(ref)

    def update(rows, slot, weight):
        mat = weight(0) * g_ref[slot, 0]
        line = weight(0) * qr_ref[slot, 0:1, :]
        for j in range(1, NBLK):
            mat = mat + weight(j) * g_ref[slot, j]
            line = line + weight(j) * qr_ref[slot, j : j + 1, :]
        move = jnp.sum(rows * line, axis=1, keepdims=True)
        return mm3(rows, mat), jnp.broadcast_to(move, (rows.shape[0], B))

    def own_steps(k, slot):
        first = order_ref[k] * NBLK

        def state(i):
            sl = slice(i * B, i * B + B)
            rows = xo_ref[sl, :]
            delta, move = update(rows, slot, lambda j: levels_ref[stape_ref[i, first + j]])
            xo_ref[sl, :] = rows - delta
            dm_ref[sl, :] = dm_ref[sl, :] + move

        def observed(q):
            sl = slice(q * PIECE, q * PIECE + PIECE)
            rows = obso_ref[sl, :]
            delta, move = update(rows, slot, lambda j: levels_ref[otape_ref[q * NBLK + mine_ref[0], first + j]])
            obso_ref[sl, :] = rows - delta
            do_ref[sl, :] = do_ref[sl, :] + move

        steps = [lambda i=i: state(i) for i in range(x_ref.shape[0] // B)]
        return steps + [lambda q=q: observed(q) for q in range(KB)]

    def batch_step(k, outer):
        slot = k % 2
        s_ref[:, :N] = mm(y_ref[k], y_ref[k], 1, 1) * (1.0 / (M - 1))
        s_ref[:, N:] = d_ref[k]
        for b in range(NBLK):
            sl = slice(b * B, b * B + B)
            s_ref[sl, sl] = s_ref[sl, sl] + jnp.where(eye, r_ref[k, sl, :], 0.0)

        def block_step(b, carry):
            at = pl.multiple_of(b * B, B)
            a_ref[:, :B] = s_ref[pl.ds(at, B), pl.ds(at, B)]
            a_ref[:, B:] = jnp.where(eye, 1.0, 0.0)
            last = jnp.maximum(b - 1, 0)
            seen = pl.multiple_of(last * B, B)
            steps = doubling_steps(
                lambda: u_ref[pl.ds(seen, B), pl.ds(seen, B)], low_ref, x8_ref.at[last], mid_ref
            )
            steps += forward_steps(
                lambda: u_ref[:, pl.ds(seen, B)], lambda: y_ref[k, pl.ds(seen, B), :],
                v_ref, v_ref.at[pl.ds(seen, B)], x8_ref.at[last], part_ref, seen,
            )
            hooks = {g + 1: step for g, step in enumerate(steps)}
            factor_block(a_ref, p_ref, w_ref.at[b], e_ref.at[k, pl.ds(at, B)], x8_ref.at[BASE], n_ref, k_ref, hooks)
            x8_ref[b] = x8_ref[BASE]
            inv = w_ref[b]
            row = mm(inv, s_ref[pl.ds(at, B), :])
            u_ref[pl.ds(at, B), :] = row
            for c in range(NBLK - 1):
                @pl.when(b == c)
                def _():
                    lo = (c + 1) * B
                    q = mm(inv, u_ref[lo - B : lo, lo:], 0, 0)
                    q_ref[lo - B : lo, lo:] = q
                    s_ref[lo:, lo:] = s_ref[lo:, lo:] - mm(s_ref[lo:, lo - B : lo], q)
            return carry

        lax.fori_loop(0, NBLK, block_step, 0)

        tail = (NBLK - 1) * B
        solving = doubling_steps(
            lambda: u_ref[tail : tail + B, tail : tail + B], low_ref, x8_ref.at[NBLK - 1], mid_ref
        )
        above, solve = forward_steps(
            lambda: u_ref[:, tail:N], lambda: y_ref[k, tail:N, :],
            v_ref, v_ref.at[tail:N], x8_ref.at[NBLK - 1], part_ref, tail,
        )
        owed = own_steps(jnp.maximum(k - 1, 0), 1 - slot)
        above()
        while solving or owed:
            if solving:
                solving.pop(0)()
            if owed:
                owed.pop(0)()
        for b in range(NBLK - 1):
            sl = slice(b * B, b * B + B)
            z_ref[sl, :M] = mm(w_ref[b], v_ref[sl, :], 0, 0)
            z_ref[sl, M:] = q_ref[sl, N:]
        solve()
        z_ref[tail:N, :M] = mm(w_ref[NBLK - 1], v_ref[tail:N, :], 0, 0)
        z_ref[tail:N, M:] = mm(w_ref[NBLK - 1], u_ref[tail:N, N:], 0, 0)
        for b in range(NBLK - 2, -1, -1):
            sl = slice(b * B, b * B + B)
            hi = (b + 1) * B
            z_ref[sl, :] = z_ref[sl, :] - mm(q_ref[sl, hi:N], z_ref[hi:N, :])
        for b in range(NBLK):
            sl = slice(b * B, b * B + B)
            g_ref[slot, b] = mm3(y_ref[k, sl, :], z_ref[sl, :M], 0, 0) * (1.0 / (M - 1))
            line = jnp.sum(y_ref[k, sl, :] * wide(z_ref[sl, M:]), axis=0, keepdims=True)
            qr_ref[slot, b : b + 1, :] = line * (1.0 / (M - 1))

        def cross_step(n, carry):
            later, i = n // NBLK, n % NBLK
            at = pl.multiple_of(i * B, B)

            def weight(j):
                line = c_ref[pl.ds(later * pairs + k * (NBLK * NBLK) + i * NBLK + j, 1), :]
                return jnp.concatenate([line] * (M // B), axis=1)

            rows = y_ref[later, pl.ds(at, B), :]
            delta, move = update(rows, slot, weight)
            y_ref[later, pl.ds(at, B), :] = rows - delta
            d_ref[later, pl.ds(at, B), :] = d_ref[later, pl.ds(at, B), :] - move
            return carry

        lax.fori_loop((k + 1) * NBLK, NB * NBLK, cross_step, 0)
        return outer

    lax.fori_loop(0, NB, batch_step, 0)
    for step in own_steps(NB - 1, (NB - 1) % 2):
        step()

    for i in range(x_ref.shape[0] // B):
        sl = slice(i * B, i * B + B)
        add = jnp.sum(jnp.where(eye, dm_ref[sl, :], 0.0), axis=0, keepdims=True)
        meano_ref[i : i + 1, :] = mean_ref[i : i + 1, :] + add
    for q in range(KB):
        sl = slice(q * PIECE, q * PIECE + PIECE)
        sub = jnp.sum(jnp.where(piece_eye, do_ref[sl, :], 0.0), axis=0, keepdims=True)
        depo_ref[q : q + 1, :] = sub


def analysis(order, levels, stape, otape, mine, one, two, x, mean, obs):
    shape = lambda *dims: jax.ShapeDtypeStruct(dims, F32)
    scratch = lambda *dims: pltpu.VMEM(dims, F32)
    vmem = pl.BlockSpec(memory_space=pltpu.VMEM)
    rows = x.shape[0]
    return pl.pallas_call(
        analysis_kernel,
        out_shape=[shape(rows, M), shape(rows // B, B), shape(KB * PIECE, M), shape(KB, B)],
        in_specs=[pl.BlockSpec(memory_space=pltpu.SMEM)] * 5 + [vmem] * 5,
        out_specs=[vmem] * 4,
        scratch_shapes=[
            scratch(NB, N, M),
            scratch(NB, N, B),
            scratch(NB, N, B),
            scratch(NB * NB * NBLK * NBLK, B),
            scratch(N, N + B),
            scratch(N, N + B),
            scratch(NBLK, B, B),
            scratch(B, 2 * B),
            scratch(B, 2 * B),
            scratch(N, M),
            scratch(2, NBLK, M, M),
            scratch(rows, B),
            scratch(KB * PIECE, B),
            scratch(NB, N, B),
            scratch(NBLK + 1, B, B),
            scratch(B, B),
            scratch(B, B),
            scratch(2, 8, M),
            scratch(16, B),
            scratch(2 * 64, B),
            scratch(N, N + B),
            scratch(B, M),
            scratch(N, WIDE),
        ],
        name="analysis",
    )(order, levels, stape, otape, mine, one, two, x, mean, obs)


ROWS = 104


def prepare_kernel(order_ref, levels_ref, otape_ref, obs_ref, dep_ref, var_ref, out_ref):
    local = [order_ref[k] % KB for k in range(NB)]
    out_ref[0:32, :] = obs_ref[local[0]]
    out_ref[48:80, :] = obs_ref[local[1]]
    out_ref[80:104, :] = obs_ref[local[2], 0:24, :]
    out_ref[40:48, :] = obs_ref[local[2], 24:32, :]
    out_ref[32:40, :] = jnp.zeros((8, M), F32)
    lane = iota((1, B), 1)
    for k in range(NB):
        line = jnp.zeros((1, B), F32)
        for b in range(NB):
            for i in range(NBLK):
                for j in range(NBLK):
                    weight = levels_ref[otape_ref[local[k] * NBLK + i, order_ref[b] * NBLK + j]]
                    line = jnp.where(lane == 2 * PIECE + (b * NBLK + i) * NBLK + j, weight, line)
        out_ref[32 + k : 33 + k, :B] = line
        for q in range(KB):
            @pl.when(local[k] == q)
            def _():
                out_ref[32 + k : 33 + k, 0:PIECE] = dep_ref[q : q + 1, :]
                out_ref[32 + k : 33 + k, PIECE : 2 * PIECE] = var_ref[q : q + 1, :]


def prepare(order, levels, otape, obs, dep, var):
    vmem = pl.BlockSpec(memory_space=pltpu.VMEM)
    return pl.pallas_call(
        prepare_kernel,
        out_shape=jax.ShapeDtypeStruct((ROWS, M), F32),
        in_specs=[pl.BlockSpec(memory_space=pltpu.SMEM)] * 3 + [vmem] * 3,
        out_specs=vmem,
        name="prepare",
    )(order, levels, otape, obs, dep, var)


def spread(block, roots, axis, size):
    place = lax.axis_index(axis)
    away = [(place - roots[k] + size) % size for k in range(NB)]
    row = iota(block.shape, 0)
    second = (row == 33) | ((row >= 48) & (row < 80))
    third = (row == 34) | ((row >= 40) & (row < 48)) | (row >= 80)
    far = jnp.where(second, away[1], jnp.where(third, away[2], away[0]))
    step = size // 2
    while step:
        moved = lax.ppermute(block, axis, [(i, (i + step) % size) for i in range(size)])
        block = jnp.where(far % (2 * step) == 0, block, moved)
        step //= 2
    return block


def per_device(state_anom, state_mean, obs_anom, obs_depart, obs_var, taper_levels, state_taper, obs_taper, batch_order):
    shard = lax.axis_index("z") * CS + lax.axis_index("c")
    owner = batch_order // KB
    payload = prepare(batch_order, taper_levels, obs_taper, obs_anom, obs_depart, obs_var)
    payload = spread(payload, owner // YS, "x", XS)
    payload = spread(payload, owner % YS, "y", YS)
    one = lax.all_gather(payload[:48], ("z", "c"))
    two = lax.all_gather(payload[48:], ("z", "c"))
    mine = (shard * PIECE // B).astype(jnp.int32).reshape(1)
    rows = state_anom.shape[0]
    anomaly, mean, obs_now, moved = analysis(
        batch_order, taper_levels, state_taper, obs_taper, mine, one, two,
        state_anom, state_mean.reshape(rows // B, B), obs_anom.reshape(KB * PIECE, M),
    )
    return (
        anomaly,
        mean.reshape(rows),
        obs_now.reshape(obs_anom.shape),
        obs_depart - moved[:, :PIECE],
    )


def solution(mesh):
    fine = Mesh(mesh.devices.reshape(XS, YS, ZS, CS), ("x", "y", "z", "c")) if hasattr(mesh, "devices") else mesh
    region, shard, both = ("x", "y"), ("z", "c"), ("x", "y", "z", "c")
    placed = (
        P(both, None),
        P(both),
        P(region, shard, None),
        P(region, shard),
        P(region, shard),
        P(),
        P(both, None),
        P(region, None),
        P(),
    )
    return jax.shard_map(
        per_device,
        mesh=fine,
        in_specs=placed,
        out_specs=(P(both, None), P(both), P(region, shard, None), P(region, shard)),
        check_vma=False,
    )
```

```python
import jax
import jax.numpy as jnp
from jax import lax
from jax.experimental import pallas as pl
from jax.experimental.pallas import tpu as pltpu
from jax.sharding import Mesh, PartitionSpec as P

M = 256
N = 512
B = 128
NBLK = N // B
NB = 3
KB = 2
XS, YS, ZS, CS = 4, 8, 8, 2
PIECE = 32
WIDE = M + B
HI = lax.Precision.HIGHEST
F32 = jnp.float32


def mm(a, b, ca=1, cb=0):
    return lax.dot_general(a, b, (((ca,), (cb,)), ((), ())), precision=HI, preferred_element_type=F32)


def halves(v):
    hi = v.astype(jnp.bfloat16)
    return hi, (v - hi.astype(F32)).astype(jnp.bfloat16)


def mm3(a, b, ca=1, cb=0):
    dot = lambda p, q: lax.dot_general(p, q, (((ca,), (cb,)), ((), ())), preferred_element_type=F32)
    (ah, al), (bh, bl) = halves(a), halves(b)
    return dot(ah, bh) + (dot(ah, bl) + dot(al, bh))


def iota(shape, axis):
    return lax.broadcasted_iota(jnp.int32, shape, axis)


def wide(v):
    return jnp.concatenate([v, v], axis=1)


def split(v):
    hi = v.astype(jnp.bfloat16)
    rest = v - hi.astype(F32)
    mid = rest.astype(jnp.bfloat16)
    return hi, mid, (rest - mid.astype(F32)).astype(jnp.bfloat16)


def factor_block(a_ref, p_ref, w_ref, root_ref, base_ref, n_ref, c_ref, hooks):
    groups = B // 8
    lane = iota((8, B), 1)
    rows = [jnp.broadcast_to(a_ref[s : s + 1, :], (8, 2 * B)) for s in range(8)]
    corner = a_ref[0:8, :B]
    for g in range(groups):
        j0 = 8 * g
        slot = 64 * (g % 2)
        for t in range(8):
            c_ref[slot + 8 * t : slot + 8 * t + 8, :] = jnp.broadcast_to(corner[:, j0 + t : j0 + t + 1], (8, B))
        d = {}
        for s in range(8):
            for t in range(s + 1):
                at = slot + 8 * t + s
                d[s, t] = jnp.broadcast_to(c_ref[at : at + 1, :], (8, B))
        low, diag = {}, []
        for t in range(8):
            inv = lax.rsqrt(d[t, t])
            diag.append(d[t, t] * inv)
            done = rows[t] * wide(inv)
            for s in range(t + 1, 8):
                low[s, t] = d[s, t] * inv
            for s in range(t + 1, 8):
                for v in range(t + 1, s + 1):
                    d[s, v] = d[s, v] - low[s, t] * low[v, t]
            for s in range(t + 1, 8):
                rows[s] = rows[s] - wide(low[s, t]) * done
            w_ref[j0 + t : j0 + t + 1, :] = done[:1, B:]
            if g < groups - 1:
                p_ref[j0 + t : j0 + t + 1, :] = done[:1, :]
        if g < groups - 1:
            panel = p_ref[j0 : j0 + 8, :]
            ahead = []
            turn = 8 * (g % 2)
            for s in range(8):
                j1 = j0 + 8 + s
                fix = wide(jnp.broadcast_to(panel[:, j1 : j1 + 1], (8, B))) * panel
                for step in (4, 2, 1):
                    fix = fix + pltpu.roll(fix, step, 0)
                ahead.append(jnp.broadcast_to(a_ref[j1 : j1 + 1, :], (8, 2 * B)) - fix)
                n_ref[turn + s : turn + s + 1, :] = ahead[s][:1, :B]
            corner = n_ref[turn : turn + 8, :]
        small = []
        for s in range(8):
            row = jnp.where(lane == j0 + s, 1.0, 0.0)
            for t in range(s):
                row = row - low[s, t] * small[t]
            shift = jnp.broadcast_to(root_ref[j0 + s : j0 + s + 1, :], (8, B))
            small.append(row * (1.0 / (diag[s] + shift)))
            base_ref[j0 + s : j0 + s + 1, :] = small[s][:1, :]
        if hooks.get(g):
            hooks[g]()
        if g == groups - 1:
            break
        rows = ahead
        lo = j0 + 16
        if lo < B:
            hi, mid, rest = split(p_ref[j0 : j0 + 8, :])
            left = jnp.concatenate([hi, hi, hi, mid, mid, rest])[:, :B]
            right = jnp.concatenate([hi, mid, rest, hi, mid, hi])
            fix = lax.dot_general(left, right, (((0,), (0,)), ((), ())), preferred_element_type=F32)
            a_ref[lo:, :] = a_ref[lo:, :] - fix[lo:, :]

def doubling_steps(u, low_ref, x_ref, mid_ref):
    ri, ci = iota((B, B), 0), iota((B, B), 1)

    def first():
        low_ref[...] = jnp.transpose(u())

    def half(m):
        mask = (ri // (2 * m) == ci // (2 * m)) & ((ri // m) % 2 == 1) & ((ci // m) % 2 == 0)
        mid_ref[...] = mm(jnp.where(mask, low_ref[...], 0.0), x_ref[...])

    def full():
        x_ref[...] = x_ref[...] - mm(x_ref[...], mid_ref[...])

    steps = [first]
    for m in (8, 16, 32, 64):
        steps += [lambda m=m: half(m), full]
    return steps


def forward_steps(cols, y, v_ref, out_ref, x_ref, part_ref, first_row):
    def above():
        factor = jnp.where(iota((N, B), 0) < first_row, cols(), 0.0)
        part_ref[...] = y() - mm(factor, v_ref[:, :M], 0, 0)

    def solve():
        out_ref[...] = mm(x_ref[...], part_ref[...])

    return [above, solve]


BASE = NBLK


def analysis_kernel(
    order_ref, levels_ref, stape_ref, otape_ref, mine_ref, one_ref, two_ref, x_ref, mean_ref, obs_ref, dep_ref,
    xo_ref, meano_ref, obso_ref, depo_ref,
    y_ref, d_ref, r_ref, c_ref, s_ref, u_ref, w_ref, a_ref, p_ref, v_ref, g_ref, dm_ref, do_ref, e_ref, x8_ref, low_ref, mid_ref, qr_ref, n_ref, k_ref, q_ref, part_ref, z_ref,
):
    eye = iota((B, B), 0) == iota((B, B), 1)
    piece_eye = iota((PIECE, B), 0) == iota((PIECE, B), 1)
    var_eye = iota((PIECE, B), 0) + PIECE == iota((PIECE, B), 1)
    pairs = NB * NBLK * NBLK
    pair_eye = iota((pairs, B), 0) + 2 * PIECE == iota((pairs, B), 1)

    def column(line, mask):
        col = jnp.sum(jnp.where(mask, line, 0.0), axis=1, keepdims=True)
        return jnp.broadcast_to(col, mask.shape)

    def unpack(s, carry):
        at = pl.multiple_of(s * PIECE, PIECE)
        y_ref[0, pl.ds(at, 32), :] = one_ref[s, 0:32, :]
        y_ref[1, pl.ds(at, 32), :] = two_ref[s, 0:32, :]
        y_ref[2, pl.ds(at, 24), :] = two_ref[s, 32:56, :]
        y_ref[2, pl.ds(at + 24, 8), :] = one_ref[s, 40:48, :]
        for k in range(NB):
            line = one_ref[s, 32 + k : 33 + k, :B]
            d_ref[k, pl.ds(at, PIECE), :] = column(line, piece_eye)
            r_ref[k, pl.ds(at, PIECE), :] = column(line, var_eye)
            e_ref[k, pl.ds(at, PIECE), :] = column(jnp.sqrt(jnp.maximum(line, 0.0)), var_eye)
        return carry

    lax.fori_loop(0, ZS * CS, unpack, 0)
    for k in range(NB):
        c_ref[k * pairs : k * pairs + pairs, :] = column(one_ref[0, 32 + k : 33 + k, :B], pair_eye)
    xo_ref[...] = x_ref[...]
    obso_ref[...] = obs_ref[...]
    dm_ref[...] = jnp.zeros_like(dm_ref)
    do_ref[...] = jnp.zeros_like(do_ref)
    for ref in (u_ref, x8_ref, v_ref, g_ref, qr_ref):
        ref[...] = jnp.zeros_like(ref)

    def update(rows, slot, weight):
        mat = weight(0) * g_ref[slot, 0]
        line = weight(0) * qr_ref[slot, 0:1, :]
        for j in range(1, NBLK):
            mat = mat + weight(j) * g_ref[slot, j]
            line = line + weight(j) * qr_ref[slot, j : j + 1, :]
        move = jnp.sum(rows * line, axis=1, keepdims=True)
        return mm3(rows, mat), jnp.broadcast_to(move, (rows.shape[0], B))

    def own_steps(k, slot):
        first = order_ref[k] * NBLK

        def state(i):
            sl = slice(i * B, i * B + B)
            rows = xo_ref[sl, :]
            delta, move = update(rows, slot, lambda j: levels_ref[stape_ref[i, first + j]])
            xo_ref[sl, :] = rows - delta
            dm_ref[sl, :] = dm_ref[sl, :] + move

        def observed(q):
            sl = slice(q * PIECE, q * PIECE + PIECE)
            rows = obso_ref[sl, :]
            delta, move = update(rows, slot, lambda j: levels_ref[otape_ref[q * NBLK + mine_ref[0], first + j]])
            obso_ref[sl, :] = rows - delta
            do_ref[sl, :] = do_ref[sl, :] + move

        steps = [lambda i=i: state(i) for i in range(x_ref.shape[0] // B)]
        return steps + [lambda q=q: observed(q) for q in range(KB)]

    def batch_step(k, outer):
        slot = k % 2
        s_ref[:, :N] = mm(y_ref[k], y_ref[k], 1, 1) * (1.0 / (M - 1))
        s_ref[:, N:] = d_ref[k]
        for b in range(NBLK):
            sl = slice(b * B, b * B + B)
            s_ref[sl, sl] = s_ref[sl, sl] + jnp.where(eye, r_ref[k, sl, :], 0.0)

        def block_step(b, carry):
            at = pl.multiple_of(b * B, B)
            a_ref[:, :B] = s_ref[pl.ds(at, B), pl.ds(at, B)]
            a_ref[:, B:] = jnp.where(eye, 1.0, 0.0)
            last = jnp.maximum(b - 1, 0)
            seen = pl.multiple_of(last * B, B)
            steps = doubling_steps(
                lambda: u_ref[pl.ds(seen, B), pl.ds(seen, B)], low_ref, x8_ref.at[last], mid_ref
            )
            steps += forward_steps(
                lambda: u_ref[:, pl.ds(seen, B)], lambda: y_ref[k, pl.ds(seen, B), :],
                v_ref, v_ref.at[pl.ds(seen, B)], x8_ref.at[last], part_ref, seen,
            )
            hooks = {g + 1: step for g, step in enumerate(steps)}
            factor_block(a_ref, p_ref, w_ref.at[b], e_ref.at[k, pl.ds(at, B)], x8_ref.at[BASE], n_ref, k_ref, hooks)
            x8_ref[b] = x8_ref[BASE]
            inv = w_ref[b]
            row = mm(inv, s_ref[pl.ds(at, B), :])
            u_ref[pl.ds(at, B), :] = row
            for c in range(NBLK - 1):
                @pl.when(b == c)
                def _():
                    lo = (c + 1) * B
                    q = mm(inv, u_ref[lo - B : lo, lo:], 0, 0)
                    q_ref[lo - B : lo, lo:] = q
                    s_ref[lo:, lo:] = s_ref[lo:, lo:] - mm(s_ref[lo:, lo - B : lo], q)
            return carry

        lax.fori_loop(0, NBLK, block_step, 0)

        tail = (NBLK - 1) * B
        solving = doubling_steps(
            lambda: u_ref[tail : tail + B, tail : tail + B], low_ref, x8_ref.at[NBLK - 1], mid_ref
        )
        above, solve = forward_steps(
            lambda: u_ref[:, tail:N], lambda: y_ref[k, tail:N, :],
            v_ref, v_ref.at[tail:N], x8_ref.at[NBLK - 1], part_ref, tail,
        )
        owed = own_steps(jnp.maximum(k - 1, 0), 1 - slot)
        above()
        while solving or owed:
            if solving:
                solving.pop(0)()
            if owed:
                owed.pop(0)()
        for b in range(NBLK - 1):
            sl = slice(b * B, b * B + B)
            z_ref[sl, :M] = mm(w_ref[b], v_ref[sl, :], 0, 0)
            z_ref[sl, M:] = q_ref[sl, N:]
        solve()
        z_ref[tail:N, :M] = mm(w_ref[NBLK - 1], v_ref[tail:N, :], 0, 0)
        z_ref[tail:N, M:] = mm(w_ref[NBLK - 1], u_ref[tail:N, N:], 0, 0)
        for b in range(NBLK - 2, -1, -1):
            sl = slice(b * B, b * B + B)
            hi = (b + 1) * B
            z_ref[sl, :] = z_ref[sl, :] - mm(q_ref[sl, hi:N], z_ref[hi:N, :])
        for b in range(NBLK):
            sl = slice(b * B, b * B + B)
            g_ref[slot, b] = mm3(y_ref[k, sl, :], z_ref[sl, :M], 0, 0) * (1.0 / (M - 1))
            line = jnp.sum(y_ref[k, sl, :] * wide(z_ref[sl, M:]), axis=0, keepdims=True)
            qr_ref[slot, b : b + 1, :] = line * (1.0 / (M - 1))

        def cross_step(n, carry):
            later, i = n // NBLK, n % NBLK
            at = pl.multiple_of(i * B, B)

            def weight(j):
                line = c_ref[pl.ds(later * pairs + k * (NBLK * NBLK) + i * NBLK + j, 1), :]
                return jnp.concatenate([line] * (M // B), axis=1)

            rows = y_ref[later, pl.ds(at, B), :]
            delta, move = update(rows, slot, weight)
            y_ref[later, pl.ds(at, B), :] = rows - delta
            d_ref[later, pl.ds(at, B), :] = d_ref[later, pl.ds(at, B), :] - move
            return carry

        lax.fori_loop((k + 1) * NBLK, NB * NBLK, cross_step, 0)
        return outer

    lax.fori_loop(0, NB, batch_step, 0)
    for step in own_steps(NB - 1, (NB - 1) % 2):
        step()

    for i in range(x_ref.shape[0] // B):
        sl = slice(i * B, i * B + B)
        add = jnp.sum(jnp.where(eye, dm_ref[sl, :], 0.0), axis=0, keepdims=True)
        meano_ref[i : i + 1, :] = mean_ref[i : i + 1, :] + add
    for q in range(KB):
        sl = slice(q * PIECE, q * PIECE + PIECE)
        sub = jnp.sum(jnp.where(piece_eye, do_ref[sl, :], 0.0), axis=0, keepdims=True)
        depo_ref[q : q + 1, :] = dep_ref[q : q + 1, :] - sub[:, :PIECE]


def analysis(order, levels, stape, otape, mine, one, two, x, mean, obs, dep):
    shape = lambda *dims: jax.ShapeDtypeStruct(dims, F32)
    scratch = lambda *dims: pltpu.VMEM(dims, F32)
    vmem = pl.BlockSpec(memory_space=pltpu.VMEM)
    rows = x.shape[0]
    return pl.pallas_call(
        analysis_kernel,
        out_shape=[shape(rows, M), shape(rows // B, B), shape(KB * PIECE, M), shape(KB, PIECE)],
        in_specs=[pl.BlockSpec(memory_space=pltpu.SMEM)] * 5 + [vmem] * 6,
        out_specs=[vmem] * 4,
        scratch_shapes=[
            scratch(NB, N, M),
            scratch(NB, N, B),
            scratch(NB, N, B),
            scratch(NB * NB * NBLK * NBLK, B),
            scratch(N, N + B),
            scratch(N, N + B),
            scratch(NBLK, B, B),
            scratch(B, 2 * B),
            scratch(B, 2 * B),
            scratch(N, M),
            scratch(2, NBLK, M, M),
            scratch(rows, B),
            scratch(KB * PIECE, B),
            scratch(NB, N, B),
            scratch(NBLK + 1, B, B),
            scratch(B, B),
            scratch(B, B),
            scratch(2, 8, M),
            scratch(16, B),
            scratch(2 * 64, B),
            scratch(N, N + B),
            scratch(B, M),
            scratch(N, WIDE),
        ],
        name="analysis",
    )(order, levels, stape, otape, mine, one, two, x, mean, obs, dep)


ROWS = 104


def prepare_kernel(order_ref, levels_ref, otape_ref, obs_ref, dep_ref, var_ref, out_ref):
    local = [order_ref[k] % KB for k in range(NB)]
    out_ref[0:32, :] = obs_ref[local[0]]
    out_ref[48:80, :] = obs_ref[local[1]]
    out_ref[80:104, :] = obs_ref[local[2], 0:24, :]
    out_ref[40:48, :] = obs_ref[local[2], 24:32, :]
    out_ref[32:40, :] = jnp.zeros((8, M), F32)
    lane = iota((1, B), 1)
    for k in range(NB):
        line = jnp.zeros((1, B), F32)
        for b in range(NB):
            for i in range(NBLK):
                for j in range(NBLK):
                    weight = levels_ref[otape_ref[local[k] * NBLK + i, order_ref[b] * NBLK + j]]
                    line = jnp.where(lane == 2 * PIECE + (b * NBLK + i) * NBLK + j, weight, line)
        out_ref[32 + k : 33 + k, :B] = line
        for q in range(KB):
            @pl.when(local[k] == q)
            def _():
                out_ref[32 + k : 33 + k, 0:PIECE] = dep_ref[q : q + 1, :]
                out_ref[32 + k : 33 + k, PIECE : 2 * PIECE] = var_ref[q : q + 1, :]


def prepare(order, levels, otape, obs, dep, var):
    vmem = pl.BlockSpec(memory_space=pltpu.VMEM)
    return pl.pallas_call(
        prepare_kernel,
        out_shape=jax.ShapeDtypeStruct((ROWS, M), F32),
        in_specs=[pl.BlockSpec(memory_space=pltpu.SMEM)] * 3 + [vmem] * 3,
        out_specs=vmem,
        name="prepare",
    )(order, levels, otape, obs, dep, var)


def spread(block, roots, axis, size):
    place = lax.axis_index(axis)
    away = [(place - roots[k] + size) % size for k in range(NB)]
    row = iota(block.shape, 0)
    second = (row == 33) | ((row >= 48) & (row < 80))
    third = (row == 34) | ((row >= 40) & (row < 48)) | (row >= 80)
    far = jnp.where(second, away[1], jnp.where(third, away[2], away[0]))
    rounds = {
        4: [{1: (1,), -1: (3,), 2: (2,)}],
        8: [{1: (1,), -1: (7,)}, {3: (2, 3, 4), -3: (5, 6)}],
    }
    for shifts in rounds[size]:
        moved = {n: lax.ppermute(block, axis, [(i, (i + n) % size) for i in range(size)]) for n in shifts}
        for n, reached in shifts.items():
            take = far == reached[0]
            for distance in reached[1:]:
                take = take | (far == distance)
            block = jnp.where(take, moved[n], block)
    return block


def per_device(state_anom, state_mean, obs_anom, obs_depart, obs_var, taper_levels, state_taper, obs_taper, batch_order):
    shard = lax.axis_index("z") * CS + lax.axis_index("c")
    owner = batch_order // KB
    payload = prepare(batch_order, taper_levels, obs_taper, obs_anom, obs_depart, obs_var)
    payload = spread(payload, owner // YS, "x", XS)
    payload = spread(payload, owner % YS, "y", YS)
    one = lax.all_gather(payload[:48], ("z", "c"))
    two = lax.all_gather(payload[48:], ("z", "c"))
    mine = (shard * PIECE // B).astype(jnp.int32).reshape(1)
    rows = state_anom.shape[0]
    anomaly, mean, obs_now, depart = analysis(
        batch_order, taper_levels, state_taper, obs_taper, mine, one, two,
        state_anom, state_mean.reshape(rows // B, B), obs_anom.reshape(KB * PIECE, M), obs_depart,
    )
    return (
        anomaly,
        mean.reshape(rows),
        obs_now.reshape(obs_anom.shape),
        depart,
    )


def solution(mesh):
    fine = Mesh(mesh.devices.reshape(XS, YS, ZS, CS), ("x", "y", "z", "c")) if hasattr(mesh, "devices") else mesh
    region, shard, both = ("x", "y"), ("z", "c"), ("x", "y", "z", "c")
    placed = (
        P(both, None),
        P(both),
        P(region, shard, None),
        P(region, shard),
        P(region, shard),
        P(),
        P(both, None),
        P(region, None),
        P(),
    )
    return jax.shard_map(
        per_device,
        mesh=fine,
        in_specs=placed,
        out_specs=(P(both, None), P(both), P(region, shard, None), P(region, shard)),
        check_vma=False,
    )
```

```python
import jax
import jax.numpy as jnp
from jax import lax
from jax.experimental import pallas as pl
from jax.experimental.pallas import tpu as pltpu
from jax.sharding import Mesh, PartitionSpec as P

M = 256
N = 512
B = 128
NBLK = N // B
NB = 3
KB = 2
XS, YS, ZS, CS = 4, 8, 8, 2
PIECE = 32
WIDE = M + B
HI = lax.Precision.HIGHEST
F32 = jnp.float32


def mm(a, b, ca=1, cb=0):
    return lax.dot_general(a, b, (((ca,), (cb,)), ((), ())), precision=HI, preferred_element_type=F32)


def halves(v):
    hi = v.astype(jnp.bfloat16)
    return hi, (v - hi.astype(F32)).astype(jnp.bfloat16)


def mm3(a, b, ca=1, cb=0):
    dot = lambda p, q: lax.dot_general(p, q, (((ca,), (cb,)), ((), ())), preferred_element_type=F32)
    (ah, al), (bh, bl) = halves(a), halves(b)
    return dot(ah, bh) + (dot(ah, bl) + dot(al, bh))


def iota(shape, axis):
    return lax.broadcasted_iota(jnp.int32, shape, axis)


def wide(v):
    return jnp.concatenate([v, v], axis=1)


def split(v):
    hi = v.astype(jnp.bfloat16)
    rest = v - hi.astype(F32)
    mid = rest.astype(jnp.bfloat16)
    return hi, mid, (rest - mid.astype(F32)).astype(jnp.bfloat16)


def factor_block(a_ref, p_ref, w_ref, root_ref, base_ref, n_ref, c_ref, hooks):
    groups = B // 8
    lane = iota((8, B), 1)
    rows = [jnp.broadcast_to(a_ref[s : s + 1, :], (8, 2 * B)) for s in range(8)]
    corner = a_ref[0:8, :B]
    for g in range(groups):
        j0 = 8 * g
        slot = 64 * (g % 2)
        for t in range(8):
            c_ref[slot + 8 * t : slot + 8 * t + 8, :] = jnp.broadcast_to(corner[:, j0 + t : j0 + t + 1], (8, B))
        d = {}
        for s in range(8):
            for t in range(s + 1):
                at = slot + 8 * t + s
                d[s, t] = jnp.broadcast_to(c_ref[at : at + 1, :], (8, B))
        low, diag = {}, []
        for t in range(8):
            inv = lax.rsqrt(d[t, t])
            diag.append(d[t, t] * inv)
            done = rows[t] * wide(inv)
            for s in range(t + 1, 8):
                low[s, t] = d[s, t] * inv
            for s in range(t + 1, 8):
                for v in range(t + 1, s + 1):
                    d[s, v] = d[s, v] - low[s, t] * low[v, t]
            for s in range(t + 1, 8):
                rows[s] = rows[s] - wide(low[s, t]) * done
            w_ref[j0 + t : j0 + t + 1, :] = done[:1, B:]
            if g < groups - 1:
                p_ref[j0 + t : j0 + t + 1, :] = done[:1, :]
        if g < groups - 1:
            panel = p_ref[j0 : j0 + 8, :]
            ahead = []
            turn = 8 * (g % 2)
            for s in range(8):
                j1 = j0 + 8 + s
                fix = wide(jnp.broadcast_to(panel[:, j1 : j1 + 1], (8, B))) * panel
                for step in (4, 2, 1):
                    fix = fix + pltpu.roll(fix, step, 0)
                ahead.append(jnp.broadcast_to(a_ref[j1 : j1 + 1, :], (8, 2 * B)) - fix)
                n_ref[turn + s : turn + s + 1, :] = ahead[s][:1, :B]
            corner = n_ref[turn : turn + 8, :]
        small = []
        for s in range(8):
            row = jnp.where(lane == j0 + s, 1.0, 0.0)
            for t in range(s):
                row = row - low[s, t] * small[t]
            shift = jnp.broadcast_to(root_ref[j0 + s : j0 + s + 1, :], (8, B))
            small.append(row * (1.0 / (diag[s] + shift)))
            base_ref[j0 + s : j0 + s + 1, :] = small[s][:1, :]
        if hooks.get(g):
            hooks[g]()
        if g == groups - 1:
            break
        rows = ahead
        lo = j0 + 16
        if lo < B:
            hi, mid, rest = split(p_ref[j0 : j0 + 8, :])
            left = jnp.concatenate([hi, hi, hi, mid, mid, rest])[:, :B]
            right = jnp.concatenate([hi, mid, rest, hi, mid, hi])
            fix = lax.dot_general(left, right, (((0,), (0,)), ((), ())), preferred_element_type=F32)
            a_ref[lo:, :] = a_ref[lo:, :] - fix[lo:, :]

def doubling_steps(u, low_ref, x_ref, mid_ref):
    ri, ci = iota((B, B), 0), iota((B, B), 1)

    def first():
        low_ref[...] = jnp.transpose(u())

    def half(m):
        mask = (ri // (2 * m) == ci // (2 * m)) & ((ri // m) % 2 == 1) & ((ci // m) % 2 == 0)
        mid_ref[...] = mm(jnp.where(mask, low_ref[...], 0.0), x_ref[...])

    def full():
        x_ref[...] = x_ref[...] - mm(x_ref[...], mid_ref[...])

    steps = [first]
    for m in (8, 16, 32, 64):
        steps += [lambda m=m: half(m), full]
    return steps


def forward_steps(cols, y, v_ref, out_ref, x_ref, part_ref, first_row):
    def above():
        factor = jnp.where(iota((N, B), 0) < first_row, cols(), 0.0)
        part_ref[...] = y() - mm(factor, v_ref[:, :M], 0, 0)

    def solve():
        out_ref[...] = mm(x_ref[...], part_ref[...])

    return [above, solve]


BASE = NBLK


def analysis_kernel(
    order_ref, levels_ref, stape_ref, otape_ref, mine_ref, one_ref, two_ref, x_ref, mean_ref, obs_ref, dep_ref,
    xo_ref, meano_ref, obso_ref, depo_ref,
    y_ref, d_ref, r_ref, c_ref, s_ref, u_ref, w_ref, a_ref, p_ref, v_ref, g_ref, dm_ref, do_ref, e_ref, x8_ref, low_ref, mid_ref, qr_ref, n_ref, k_ref, q_ref, part_ref, z_ref,
):
    eye = iota((B, B), 0) == iota((B, B), 1)
    piece_eye = iota((PIECE, B), 0) == iota((PIECE, B), 1)
    var_eye = iota((PIECE, B), 0) + PIECE == iota((PIECE, B), 1)
    pairs = NB * NBLK * NBLK
    pair_eye = iota((pairs, B), 0) + 2 * PIECE == iota((pairs, B), 1)

    def column(line, mask):
        col = jnp.sum(jnp.where(mask, line, 0.0), axis=1, keepdims=True)
        return jnp.broadcast_to(col, mask.shape)

    def unpack(s, carry):
        at = pl.multiple_of(s * PIECE, PIECE)
        y_ref[0, pl.ds(at, 32), :] = one_ref[s, 0:32, :]
        y_ref[1, pl.ds(at, 32), :] = two_ref[s, 0:32, :]
        y_ref[2, pl.ds(at, 24), :] = two_ref[s, 32:56, :]
        y_ref[2, pl.ds(at + 24, 8), :] = one_ref[s, 40:48, :]
        for k in range(NB):
            line = one_ref[s, 32 + k : 33 + k, :B]
            d_ref[k, pl.ds(at, PIECE), :] = column(line, piece_eye)
            r_ref[k, pl.ds(at, PIECE), :] = column(line, var_eye)
            e_ref[k, pl.ds(at, PIECE), :] = column(jnp.sqrt(jnp.maximum(line, 0.0)), var_eye)
        return carry

    lax.fori_loop(0, ZS * CS, unpack, 0, unroll=8)
    for k in range(NB):
        c_ref[k * pairs : k * pairs + pairs, :] = column(one_ref[0, 32 + k : 33 + k, :B], pair_eye)
    xo_ref[...] = x_ref[...]
    obso_ref[...] = obs_ref[...]
    dm_ref[...] = jnp.zeros_like(dm_ref)
    do_ref[...] = jnp.zeros_like(do_ref)
    for ref in (u_ref, x8_ref, v_ref, g_ref, qr_ref):
        ref[...] = jnp.zeros_like(ref)

    def update(rows, slot, weight):
        mat = weight(0) * g_ref[slot, 0]
        line = weight(0) * qr_ref[slot, 0:1, :]
        for j in range(1, NBLK):
            mat = mat + weight(j) * g_ref[slot, j]
            line = line + weight(j) * qr_ref[slot, j : j + 1, :]
        move = jnp.sum(rows * line, axis=1, keepdims=True)
        return mm3(rows, mat), jnp.broadcast_to(move, (rows.shape[0], B))

    def own_steps(k, slot):
        first = order_ref[k] * NBLK

        def state(i):
            sl = slice(i * B, i * B + B)
            rows = xo_ref[sl, :]
            delta, move = update(rows, slot, lambda j: levels_ref[stape_ref[i, first + j]])
            xo_ref[sl, :] = rows - delta
            dm_ref[sl, :] = dm_ref[sl, :] + move

        def observed(q):
            sl = slice(q * PIECE, q * PIECE + PIECE)
            rows = obso_ref[sl, :]
            delta, move = update(rows, slot, lambda j: levels_ref[otape_ref[q * NBLK + mine_ref[0], first + j]])
            obso_ref[sl, :] = rows - delta
            do_ref[sl, :] = do_ref[sl, :] + move

        steps = [lambda i=i: state(i) for i in range(x_ref.shape[0] // B)]
        return steps + [lambda q=q: observed(q) for q in range(KB)]

    def batch_step(k, outer):
        slot = k % 2
        s_ref[:, :N] = mm(y_ref[k], y_ref[k], 1, 1) * (1.0 / (M - 1))
        s_ref[:, N:] = d_ref[k]
        for b in range(NBLK):
            sl = slice(b * B, b * B + B)
            s_ref[sl, sl] = s_ref[sl, sl] + jnp.where(eye, r_ref[k, sl, :], 0.0)

        def block_step(b, carry):
            at = pl.multiple_of(b * B, B)
            a_ref[:, :B] = s_ref[pl.ds(at, B), pl.ds(at, B)]
            a_ref[:, B:] = jnp.where(eye, 1.0, 0.0)
            last = jnp.maximum(b - 1, 0)
            seen = pl.multiple_of(last * B, B)
            steps = doubling_steps(
                lambda: u_ref[pl.ds(seen, B), pl.ds(seen, B)], low_ref, x8_ref.at[last], mid_ref
            )
            steps += forward_steps(
                lambda: u_ref[:, pl.ds(seen, B)], lambda: y_ref[k, pl.ds(seen, B), :],
                v_ref, v_ref.at[pl.ds(seen, B)], x8_ref.at[last], part_ref, seen,
            )
            hooks = {g + 1: step for g, step in enumerate(steps)}
            factor_block(a_ref, p_ref, w_ref.at[b], e_ref.at[k, pl.ds(at, B)], x8_ref.at[BASE], n_ref, k_ref, hooks)
            x8_ref[b] = x8_ref[BASE]
            inv = w_ref[b]
            row = mm(inv, s_ref[pl.ds(at, B), :])
            u_ref[pl.ds(at, B), :] = row
            for c in range(NBLK - 1):
                @pl.when(b == c)
                def _():
                    lo = (c + 1) * B
                    q = mm(inv, u_ref[lo - B : lo, lo:], 0, 0)
                    q_ref[lo - B : lo, lo:] = q
                    s_ref[lo:, lo:] = s_ref[lo:, lo:] - mm(s_ref[lo:, lo - B : lo], q)
            return carry

        lax.fori_loop(0, NBLK, block_step, 0)

        tail = (NBLK - 1) * B
        solving = doubling_steps(
            lambda: u_ref[tail : tail + B, tail : tail + B], low_ref, x8_ref.at[NBLK - 1], mid_ref
        )
        above, solve = forward_steps(
            lambda: u_ref[:, tail:N], lambda: y_ref[k, tail:N, :],
            v_ref, v_ref.at[tail:N], x8_ref.at[NBLK - 1], part_ref, tail,
        )
        owed = own_steps(jnp.maximum(k - 1, 0), 1 - slot)
        above()
        while solving or owed:
            if solving:
                solving.pop(0)()
            if owed:
                owed.pop(0)()
        for b in range(NBLK - 1):
            sl = slice(b * B, b * B + B)
            z_ref[sl, :M] = mm(w_ref[b], v_ref[sl, :], 0, 0)
            z_ref[sl, M:] = q_ref[sl, N:]
        solve()
        z_ref[tail:N, :M] = mm(w_ref[NBLK - 1], v_ref[tail:N, :], 0, 0)
        z_ref[tail:N, M:] = mm(w_ref[NBLK - 1], u_ref[tail:N, N:], 0, 0)
        for b in range(NBLK - 2, -1, -1):
            sl = slice(b * B, b * B + B)
            hi = (b + 1) * B
            z_ref[sl, :] = z_ref[sl, :] - mm(q_ref[sl, hi:N], z_ref[hi:N, :])
        for b in range(NBLK):
            sl = slice(b * B, b * B + B)
            g_ref[slot, b] = mm3(y_ref[k, sl, :], z_ref[sl, :M], 0, 0) * (1.0 / (M - 1))
            line = jnp.sum(y_ref[k, sl, :] * wide(z_ref[sl, M:]), axis=0, keepdims=True)
            qr_ref[slot, b : b + 1, :] = line * (1.0 / (M - 1))

        def cross_step(later, carry):
            for i in range(NBLK):
                sl = slice(i * B, i * B + B)

                def weight(j):
                    line = c_ref[pl.ds(later * pairs + k * (NBLK * NBLK) + i * NBLK + j, 1), :]
                    return wide(line)

                rows = y_ref[later, sl, :]
                delta, move = update(rows, slot, weight)
                y_ref[later, sl, :] = rows - delta
                d_ref[later, sl, :] = d_ref[later, sl, :] - move
            return carry

        lax.fori_loop(k + 1, NB, cross_step, 0)
        return outer

    lax.fori_loop(0, NB, batch_step, 0)
    for step in own_steps(NB - 1, (NB - 1) % 2):
        step()

    for i in range(x_ref.shape[0] // B):
        sl = slice(i * B, i * B + B)
        add = jnp.sum(jnp.where(eye, dm_ref[sl, :], 0.0), axis=0, keepdims=True)
        meano_ref[i : i + 1, :] = mean_ref[i : i + 1, :] + add
    for q in range(KB):
        sl = slice(q * PIECE, q * PIECE + PIECE)
        sub = jnp.sum(jnp.where(piece_eye, do_ref[sl, :], 0.0), axis=0, keepdims=True)
        depo_ref[q : q + 1, :] = dep_ref[q : q + 1, :] - sub[:, :PIECE]


def analysis(order, levels, stape, otape, mine, one, two, x, mean, obs, dep):
    shape = lambda *dims: jax.ShapeDtypeStruct(dims, F32)
    scratch = lambda *dims: pltpu.VMEM(dims, F32)
    vmem = pl.BlockSpec(memory_space=pltpu.VMEM)
    rows = x.shape[0]
    return pl.pallas_call(
        analysis_kernel,
        out_shape=[shape(rows, M), shape(rows // B, B), shape(KB * PIECE, M), shape(KB, PIECE)],
        in_specs=[pl.BlockSpec(memory_space=pltpu.SMEM)] * 5 + [vmem] * 6,
        out_specs=[vmem] * 4,
        scratch_shapes=[
            scratch(NB, N, M),
            scratch(NB, N, B),
            scratch(NB, N, B),
            scratch(NB * NB * NBLK * NBLK, B),
            scratch(N, N + B),
            scratch(N, N + B),
            scratch(NBLK, B, B),
            scratch(B, 2 * B),
            scratch(B, 2 * B),
            scratch(N, M),
            scratch(2, NBLK, M, M),
            scratch(rows, B),
            scratch(KB * PIECE, B),
            scratch(NB, N, B),
            scratch(NBLK + 1, B, B),
            scratch(B, B),
            scratch(B, B),
            scratch(2, 8, M),
            scratch(16, B),
            scratch(2 * 64, B),
            scratch(N, N + B),
            scratch(B, M),
            scratch(N, WIDE),
        ],
        name="analysis",
    )(order, levels, stape, otape, mine, one, two, x, mean, obs, dep)


ROWS = 104


def prepare_kernel(order_ref, levels_ref, otape_ref, obs_ref, dep_ref, var_ref, out_ref):
    local = [order_ref[k] % KB for k in range(NB)]
    out_ref[0:32, :] = obs_ref[local[0]]
    out_ref[48:80, :] = obs_ref[local[1]]
    out_ref[80:104, :] = obs_ref[local[2], 0:24, :]
    out_ref[40:48, :] = obs_ref[local[2], 24:32, :]
    out_ref[32:40, :] = jnp.zeros((8, M), F32)
    lane = iota((1, B), 1)
    for k in range(NB):
        line = jnp.zeros((1, B), F32)
        for b in range(NB):
            for i in range(NBLK):
                for j in range(NBLK):
                    weight = levels_ref[otape_ref[local[k] * NBLK + i, order_ref[b] * NBLK + j]]
                    line = jnp.where(lane == 2 * PIECE + (b * NBLK + i) * NBLK + j, weight, line)
        out_ref[32 + k : 33 + k, :B] = line
        for q in range(KB):
            @pl.when(local[k] == q)
            def _():
                out_ref[32 + k : 33 + k, 0:PIECE] = dep_ref[q : q + 1, :]
                out_ref[32 + k : 33 + k, PIECE : 2 * PIECE] = var_ref[q : q + 1, :]


def prepare(order, levels, otape, obs, dep, var):
    vmem = pl.BlockSpec(memory_space=pltpu.VMEM)
    return pl.pallas_call(
        prepare_kernel,
        out_shape=jax.ShapeDtypeStruct((ROWS, M), F32),
        in_specs=[pl.BlockSpec(memory_space=pltpu.SMEM)] * 3 + [vmem] * 3,
        out_specs=vmem,
        name="prepare",
    )(order, levels, otape, obs, dep, var)


def spread(block, roots, axis, size):
    place = lax.axis_index(axis)
    away = [(place - roots[k] + size) % size for k in range(NB)]
    row = iota(block.shape, 0)
    second = (row == 33) | ((row >= 48) & (row < 80))
    third = (row == 34) | ((row >= 40) & (row < 48)) | (row >= 80)
    far = jnp.where(second, away[1], jnp.where(third, away[2], away[0]))
    rounds = {
        4: [{1: (1,), -1: (3,), 2: (2,)}],
        8: [{1: (1,), -1: (7,)}, {3: (2, 3, 4), -3: (5, 6)}],
    }
    for shifts in rounds[size]:
        moved = {n: lax.ppermute(block, axis, [(i, (i + n) % size) for i in range(size)]) for n in shifts}
        for n, reached in shifts.items():
            take = far == reached[0]
            for distance in reached[1:]:
                take = take | (far == distance)
            block = jnp.where(take, moved[n], block)
    return block


def per_device(state_anom, state_mean, obs_anom, obs_depart, obs_var, taper_levels, state_taper, obs_taper, batch_order):
    shard = lax.axis_index("z") * CS + lax.axis_index("c")
    owner = batch_order // KB
    payload = prepare(batch_order, taper_levels, obs_taper, obs_anom, obs_depart, obs_var)
    payload = spread(payload, owner // YS, "x", XS)
    payload = spread(payload, owner % YS, "y", YS)
    one = lax.all_gather(payload[:48], ("z", "c"))
    two = lax.all_gather(payload[48:], ("z", "c"))
    mine = (shard * PIECE // B).astype(jnp.int32).reshape(1)
    rows = state_anom.shape[0]
    anomaly, mean, obs_now, depart = analysis(
        batch_order, taper_levels, state_taper, obs_taper, mine, one, two,
        state_anom, state_mean.reshape(rows // B, B), obs_anom.reshape(KB * PIECE, M), obs_depart,
    )
    return (
        anomaly,
        mean.reshape(rows),
        obs_now.reshape(obs_anom.shape),
        depart,
    )


def solution(mesh):
    fine = Mesh(mesh.devices.reshape(XS, YS, ZS, CS), ("x", "y", "z", "c")) if hasattr(mesh, "devices") else mesh
    region, shard, both = ("x", "y"), ("z", "c"), ("x", "y", "z", "c")
    placed = (
        P(both, None),
        P(both),
        P(region, shard, None),
        P(region, shard),
        P(region, shard),
        P(),
        P(both, None),
        P(region, None),
        P(),
    )
    return jax.shard_map(
        per_device,
        mesh=fine,
        in_specs=placed,
        out_specs=(P(both, None), P(both), P(region, shard, None), P(region, shard)),
        check_vma=False,
    )
```
